256 devices in a mesh: scen: 8 (over x, z_lo), grid: 32 (over z_hi, y, core).
Axes of the slice: x: 4, y: 4, z: 8 (z_hi: 4, z_lo: 2; z = z_hi * 2 + z_lo), core: 2. Of those that a mesh axis runs over, the one named last changes fastest.
Arguments:
- value_next: float32 [512, 64, 1024], P('grid', 'scen'), may hold values from -8 to 8
- scenario_ids: int32 [8], P('scen'), may hold values from 0 to 11
- inflow_table: int32 [12, 3], replicated, may hold values from 0 to 8, as said below
- release_shifts: int32 [16, 3], replicated, may hold values from 0 to 8, as said below
- price: float32 [3], replicated, may hold values from 0.5 to 4
Outputs:
- value_now: float32 [512, 64, 1024], P('grid', 'scen')
The draws below stay inside these ranges and needn't reach their ends.
Inputs may be any that keep to these rules, and one draw needn't show every extreme that they name: `inflow_table`: inflows lie in 0 to 8; each draw holds a 0 and an 8. `release_shifts`: releases lie in 0 to 8; one decision releases 8 from every reservoir and one releases nothing.
All inputs are finite; a program needn't handle non-finite values.
Results may differ from the reference program's by a relative error of at most 0.0003.
Values sent between devices are 32-bit elements; how exact they have to be, the bound alone decides.
A program may use at most 128 MiB of HBM per device.

```python
import math
import jax
import jax.numpy as jnp
from jax import lax

H = 8
S2 = 1024
S3 = 64
RELEASES = 16
NINFLOW = 12
S1 = 512
SCENARIOS = 8


def draw_inflow_table(key, part):
    table = jax.random.randint(jax.random.fold_in(key, 11), (NINFLOW, 3), 0, H + 1)
    spots = jax.random.randint(jax.random.fold_in(key, 12), (2,), 0, NINFLOW * 3)
    flat = table.reshape(-1)
    flat = flat.at[spots[0]].set(H)
    flat = flat.at[(spots[0] + 1 + spots[1] % (NINFLOW * 3 - 1)) % (NINFLOW * 3)].set(0)
    return flat.reshape(NINFLOW, 3).astype(jnp.int32)


def draw_release_shifts(key, part):
    table = jax.random.randint(jax.random.fold_in(key, 21), (RELEASES, 3), 0, H + 1)
    order = jax.random.permutation(jax.random.fold_in(key, 22), RELEASES)
    table = table.at[order[0]].set(jnp.full((3,), H, jnp.int32))
    table = table.at[order[1]].set(jnp.zeros((3,), jnp.int32))
    return table.astype(jnp.int32)


def set_ends(array, rng, smallest, top_value):
    longest = array.shape.index(max(array.shape))
    spots = []
    for shift in (0, 1):
        where = [jax.random.randint(jax.random.fold_in(rng, axis), (), 0, length) for axis, length in enumerate(array.shape)]
        where[longest] = (where[longest] + shift) % array.shape[longest]
        spots.append(tuple(where))
    return array.at[spots[0]].set(smallest).at[spots[1]].set(top_value)


def steps_of(rng, shape, cuts, smallest, top_value):
    level = 1.0
    for axis_at, shards_of in cuts:
        steps = jax.random.uniform(jax.random.fold_in(jax.random.fold_in(rng, 6), axis_at), (shards_of,), jnp.float32, smallest / len(cuts), top_value / len(cuts))
        level = level * jnp.repeat(jnp.exp(steps), shape[axis_at] // shards_of).reshape((-1,) + (1,) * (len(shape) - 1 - axis_at))
    return level


def bell_draw(own_key, dims, scale, limit, split=(), dtype=jnp.bfloat16):
    level = steps_of(own_key, dims, split, -0.22, 0.18) if split else 1.0
    drawn = jax.random.normal(own_key, dims, jnp.float32) * scale * level
    return jnp.minimum(jnp.maximum(drawn, -limit), limit).astype(dtype)


def setup_inputs(seed: int = 0) -> dict:
    seeds = jax.random.split(jax.random.key(seed), 6)
    value_next = bell_draw(seeds[0], (S1, S3, S2), 2.0, 8.0, ((0, 32), (1, 8)), jnp.float32)
    scenario_ids = set_ends(jax.random.randint(seeds[1], (SCENARIOS,), 0, NINFLOW), jax.random.fold_in(seeds[1], 1), 0, NINFLOW - 1).astype(jnp.int32)
    inflow_table = draw_inflow_table(jax.random.fold_in(seeds[5], 71), 0)
    release_shifts = draw_release_shifts(jax.random.fold_in(seeds[5], 71), 0)
    price = jnp.clip(jnp.exp(jax.random.uniform(seeds[4], (3,), jnp.float32, math.log(0.5), math.log(4.0))), 0.5, 4.0)
    return dict(value_next=value_next, scenario_ids=scenario_ids, inflow_table=inflow_table, release_shifts=release_shifts, price=price)


softness = 0.5


def reference(value_next, scenario_ids, inflow_table, release_shifts, price):
    wide_pad = 2 * H
    extended = jnp.pad(value_next, ((H, H), (wide_pad, wide_pad), (wide_pad, wide_pad)), mode="edge")
    height_first = ((jnp.arange(S1) + 1).astype(jnp.float32) / float(S1)).reshape(S1, 1, 1)
    height_third = ((jnp.arange(S3) + 1).astype(jnp.float32) / float(S3)).reshape(1, S3, 1)
    height_second = ((jnp.arange(S2) + 1).astype(jnp.float32) / float(S2)).reshape(1, 1, S2)

    def scenario(running_total, table_row):
        inflow = inflow_table[table_row]

        def add_release(release_index, running):
            release = release_shifts[release_index]
            first_index = (H + inflow[0] - release[0]).astype(jnp.int32)
            third_index = (wide_pad + inflow[2] + release[1] - release[2]).astype(jnp.int32)
            second_index = (wide_pad + inflow[1] + release[0] - release[1]).astype(jnp.int32)
            landed = lax.dynamic_slice(extended, (first_index, third_index, second_index), (S1, S3, S2))
            amount = release.astype(jnp.float32)
            benefit = (price[0] * amount[0] * height_first + price[1] * amount[1] * height_second + price[2] * amount[2] * height_third) / float(H)
            return running + jnp.exp(-(landed - benefit) / softness)

        running = lax.fori_loop(0, RELEASES, add_release, jnp.zeros((S1, S3, S2), jnp.float32))
        return running_total - softness * jnp.log(running), None

    running_total, _ = lax.scan(scenario, jnp.zeros((S1, S3, S2), jnp.float32), scenario_ids)
    average = running_total / float(SCENARIOS)
    return average - jnp.mean(average)
```

```python
import math

import jax
import jax.numpy as jnp
from jax import lax
from jax.experimental import pallas as pl
from jax.experimental.pallas import tpu as pltpu
from jax.sharding import PartitionSpec as P

H = 8
RELEASES = 16
SCENARIOS = 8
LANES = 128
LOG2E = 1.4426950408889634
MESH = pl.DeviceIdType.MESH


def kernel(
    dims,
    x_ref,
    id_ref,
    inflow_ref,
    release_ref,
    price_ref,
    avg_ref,
    mean_ref,
    raw,
    grown,
    own_id,
    all_ids,
    part_a,
    got_a,
    part_b,
    got_b,
    ids_s,
    base_s,
    amount_s,
    rate_s,
    local_sem,
    id_local_sem,
    send_c,
    recv_c,
    send_a,
    recv_a,
    send_id,
    recv_id,
    send_ma,
    recv_ma,
    send_mb,
    recv_mb,
):
    scen_count, grid_count, rows, depth, width = dims
    tiles = width // LANES
    total_rows = rows * grid_count
    total_depth = depth * scen_count
    span = 4 * depth
    reach = rows + 2 * H
    tile_rows = reach * span
    s = lax.axis_index("scen")
    g = lax.axis_index("grid")

    def scen_peer(step):
        return {"scen": lax.rem(s + step + scen_count, scen_count), "grid": g}

    def grid_peer(step):
        return {"scen": s, "grid": lax.rem(g + step + grid_count, grid_count)}

    own_id[...] = jnp.full((1, LANES), id_ref[0], jnp.int32)
    all_ids[s] = jnp.full((1, LANES), id_ref[0], jnp.int32)

    def lanes(i):
        return pl.ds(pl.multiple_of(i * LANES, LANES), LANES)

    def own_copy(i):
        return pltpu.make_async_copy(
            x_ref.at[:, :, lanes(i)], raw.at[i, 1, pl.ds(H, rows)], local_sem.at[i]
        )

    def scen_copy(i, which):
        step, slot = ((1, 0), (-1, 2), (-2, 3))[which]
        return pltpu.make_async_remote_copy(
            src_ref=x_ref.at[:, :, lanes(i)],
            dst_ref=raw.at[i, slot, pl.ds(H, rows)],
            send_sem=send_c.at[i, which],
            recv_sem=recv_c.at[i, which],
            device_id=scen_peer(step),
            device_id_type=MESH,
        )

    def grid_copy(i, slot, way):
        if way == 0:
            first, landing, step = 0, H + rows, -1
        else:
            first, landing, step = rows - H, 0, 1
        if slot == 1:
            source = x_ref.at[pl.ds(first, H), :, lanes(i)]
        else:
            source = raw.at[i, slot, pl.ds(H + first, H)]
        return pltpu.make_async_remote_copy(
            src_ref=source,
            dst_ref=raw.at[i, slot, pl.ds(landing, H)],
            send_sem=send_a.at[i, slot, way],
            recv_sem=recv_a.at[i, slot, way],
            device_id=grid_peer(step),
            device_id_type=MESH,
        )

    def id_copy(step):
        return pltpu.make_async_remote_copy(
            src_ref=own_id,
            dst_ref=all_ids.at[s],
            send_sem=send_id.at[step - 1],
            recv_sem=recv_id.at[step - 1],
            device_id=scen_peer(step),
            device_id_type=MESH,
        )

    def mean_a_copy(step):
        return pltpu.make_async_remote_copy(
            src_ref=part_a,
            dst_ref=got_a.at[step - 1],
            send_sem=send_ma.at[step - 1],
            recv_sem=recv_ma.at[step - 1],
            device_id=scen_peer(step),
            device_id_type=MESH,
        )

    def mean_b_copy(step):
        return pltpu.make_async_remote_copy(
            src_ref=part_b,
            dst_ref=got_b.at[step - 1],
            send_sem=send_mb.at[step - 1],
            recv_sem=recv_mb.at[step - 1],
            device_id=grid_peer(step),
            device_id_type=MESH,
        )

    def loop(start, stop, body):
        def step(i, carry):
            body(i)
            return carry

        lax.fori_loop(start, stop, step, 0)

    barrier = pltpu.get_barrier_semaphore()
    loop(
        1,
        scen_count,
        lambda k: pl.semaphore_signal(barrier, inc=1, device_id=scen_peer(k), device_id_type=MESH),
    )
    loop(
        1,
        grid_count,
        lambda k: pl.semaphore_signal(barrier, inc=1, device_id=grid_peer(k), device_id_type=MESH),
    )
    loop(0, tiles, lambda i: own_copy(i).start())
    pl.semaphore_wait(barrier, scen_count + grid_count - 2)

    loop(1, scen_count, lambda k: id_copy(k).start())

    def start_all(i):
        for which in (0, 1, 2):
            scen_copy(i, which).start()
        for way in (0, 1):
            grid_copy(i, 1, way).start()

    loop(0, tiles, start_all)

    scale = -LOG2E / 4.0

    def rates(r):
        rate_s[0, r] = (price_ref[0] * scale / total_rows) * (H - release_ref[r, 0]).astype(jnp.float32)
        rate_s[1, r] = (price_ref[1] * scale / width) * (H - release_ref[r, 1]).astype(jnp.float32)
        rate_s[2, r] = (price_ref[2] * scale / total_depth) * (H - release_ref[r, 2]).astype(jnp.float32)

    loop(0, RELEASES, rates)

    loop(1, scen_count, lambda k: id_copy(k).wait_recv())
    to_scalar = pltpu.make_async_copy(all_ids, ids_s, id_local_sem)
    to_scalar.start()
    to_scalar.wait()

    def shifts(w):
        row = ids_s[w, 0, 0]
        i1 = inflow_ref[row, 0]
        i2 = inflow_ref[row, 1]
        i3 = inflow_ref[row, 2]

        def one(r):
            u1 = release_ref[r, 0]
            u2 = release_ref[r, 1]
            u3 = release_ref[r, 2]
            along = i2 + u1 - u2
            back = jnp.where(along < 0, 1, 0)
            base_s[w, r] = (1 - back) * tile_rows + (H + i1 - u1) * span + (depth + i3 + u2 - u3)
            amount_s[w, r] = along + back * LANES

        loop(0, RELEASES, one)

    loop(0, scen_count, shifts)

    lane = lax.broadcasted_iota(jnp.int32, (depth, LANES), 1)
    level_c = (lax.broadcasted_iota(jnp.int32, (depth, LANES), 0) + s * depth + 1).astype(jnp.float32)
    level_b = (lane + 1).astype(jnp.float32)
    lowest = jnp.where(g == 0, H, 0)
    highest = jnp.where(g == grid_count - 1, H + rows - 1, reach - 1)
    at_first = s == 0
    at_last = s == scen_count - 1
    near_last = s >= scen_count - 2

    def grow(v):
        return jnp.exp2(v * (-2.0 * LOG2E))

    def build(i):
        def one_row(a):
            source = jnp.clip(a, lowest, highest)
            v0 = raw[i, 0, source]
            v1 = raw[i, 1, source]
            v2 = raw[i, 2, source]
            v3 = raw[i, 3, source]
            v0 = jnp.where(at_first, jnp.broadcast_to(v1[0:1], v0.shape), v0)
            v2 = jnp.where(at_last, jnp.broadcast_to(v1[depth - 1 : depth], v0.shape), v2)
            v3 = jnp.where(near_last, jnp.broadcast_to(v2[depth - 1 : depth], v0.shape), v3)
            at = (i + 1) * tile_rows + a * span
            for slot, v in enumerate((v0, v1, v2, v3)):
                grown[pl.ds(pl.multiple_of(at + slot * depth, depth), depth), :] = grow(v)

        loop(0, reach, one_row)

    def edge(from_tile, to_tile, column):
        def one(k):
            at = pl.multiple_of(k * depth, depth)
            v = grown[pl.ds(from_tile * tile_rows + at, depth), :]
            grown[pl.ds(to_tile * tile_rows + at, depth), :] = jnp.broadcast_to(
                v[:, column : column + 1], (depth, LANES)
            )

        loop(0, tile_rows // depth, one)

    group = 4

    def compute(j, total):
        level = level_b + (j * LANES).astype(jnp.float32)

        def one_group(q, total):
            first = q * group

            def one_release(r, sums):
                sums = list(sums)
                flat = rate_s[2, r] * level_c + rate_s[1, r] * level
                weights = []
                for k in range(group):
                    row = (g * rows + first + k + 1).astype(jnp.float32)
                    weights.append(jnp.exp2(flat + rate_s[0, r] * row))
                for w in range(SCENARIOS):
                    at = base_s[w, r] + j * tile_rows + first * span
                    amount = amount_s[w, r]
                    mask = lane < amount
                    turn = jnp.bitwise_and(LANES - amount, LANES - 1)
                    for k in range(group):
                        low = grown[pl.ds(at + k * span, depth), :]
                        high = grown[pl.ds(at + k * span + tile_rows, depth), :]
                        landed = pltpu.roll(jnp.where(mask, high, low), turn, 1)
                        sums[w * group + k] = sums[w * group + k] + weights[k] * landed
                return tuple(sums)

            zero = jnp.zeros((depth, LANES), jnp.float32)
            sums = lax.fori_loop(0, RELEASES, one_release, (zero,) * (SCENARIOS * group))
            for k in range(group):
                t = [sums[w * group + k] for w in range(SCENARIOS)]
                logs = jnp.log(t[0] * t[1] * (t[2] * t[3])) + jnp.log(t[4] * t[5] * (t[6] * t[7]))
                row = (g * rows + first + k + 1).astype(jnp.float32)
                top = (
                    (price_ref[2] / total_depth) * level_c
                    + (price_ref[1] / width) * level
                    + (price_ref[0] / total_rows) * row
                )
                value = -top - (0.5 / SCENARIOS) * logs
                avg_ref[first + k, :, lanes(j)] = value
                total = total + value
            return total

        return lax.fori_loop(0, rows // group, one_group, total)

    def finish(i):
        for slot in range(4):
            for way in (0, 1):
                grid_copy(i, slot, way).wait_recv()
        build(i)

    def step(i, total):
        own_copy(i).wait()
        for which, slot in ((0, 0), (1, 2), (2, 3)):
            scen_copy(i, which).wait_recv()
            for way in (0, 1):
                grid_copy(i, slot, way).start()

        @pl.when(i >= 1)
        def _():
            finish(i - 1)

        @pl.when(i == 1)
        def _():
            edge(1, 0, 0)

        return lax.cond(i >= 2, lambda t: compute(i - 2, t), lambda t: t, total)

    total = jnp.zeros((depth, LANES), jnp.float32)
    total = lax.fori_loop(0, tiles, step, total)
    finish(tiles - 1)
    edge(tiles, tiles + 1, LANES - 1)
    total = lax.fori_loop(tiles - 2, tiles, compute, total)

    part_a[...] = jnp.sum(total, axis=0, keepdims=True)
    loop(1, scen_count, lambda k: mean_a_copy(k).start())
    loop(1, scen_count, lambda k: mean_a_copy(k).wait_recv())
    part_b[...] = part_a[...] + jnp.sum(got_a[...], axis=0)
    loop(1, grid_count, lambda k: mean_b_copy(k).start())
    loop(1, grid_count, lambda k: mean_b_copy(k).wait_recv())
    whole = part_b[...] + jnp.sum(got_b[...], axis=0)
    cells = float(total_rows * total_depth * width)
    mean_ref[...] = jnp.broadcast_to(jnp.sum(whole, axis=1, keepdims=True) / cells, (1, LANES))

    loop(1, scen_count, lambda k: id_copy(k).wait_send())
    loop(1, scen_count, lambda k: mean_a_copy(k).wait_send())
    loop(1, grid_count, lambda k: mean_b_copy(k).wait_send())

    def drain(i):
        for which in (0, 1, 2):
            scen_copy(i, which).wait_send()
        for slot in range(4):
            for way in (0, 1):
                grid_copy(i, slot, way).wait_send()

    loop(0, tiles, drain)


def solution(mesh):
    scen_count = mesh.shape["scen"]
    grid_count = mesh.shape["grid"]

    def on_device(value_next, scenario_ids, inflow_table, release_shifts, price):
        rows, depth, width = value_next.shape
        tiles = width // LANES
        dims = (scen_count, grid_count, rows, depth, width)
        reach = rows + 2 * H
        smem = pl.BlockSpec(memory_space=pltpu.SMEM)
        vmem = pl.BlockSpec(memory_space=pltpu.VMEM)
        dma = pltpu.SemaphoreType.DMA
        average, mean = pl.pallas_call(
            lambda *refs: kernel(dims, *refs),
            out_shape=(
                jax.ShapeDtypeStruct((rows, depth, width), jnp.float32),
                jax.ShapeDtypeStruct((1, LANES), jnp.float32),
            ),
            in_specs=[pl.BlockSpec(memory_space=pl.ANY), smem, smem, smem, smem],
            out_specs=(vmem, vmem),
            scratch_shapes=[
                pltpu.VMEM((tiles, 4, reach, depth, LANES), jnp.float32),
                pltpu.VMEM(((tiles + 2) * reach * 4 * depth, LANES), jnp.float32),
                pltpu.VMEM((1, LANES), jnp.int32),
                pltpu.VMEM((scen_count, 1, LANES), jnp.int32),
                pltpu.VMEM((1, LANES), jnp.float32),
                pltpu.VMEM((scen_count - 1, 1, LANES), jnp.float32),
                pltpu.VMEM((1, LANES), jnp.float32),
                pltpu.VMEM((grid_count - 1, 1, LANES), jnp.float32),
                pltpu.SMEM((scen_count, 1, LANES), jnp.int32),
                pltpu.SMEM((SCENARIOS, RELEASES), jnp.int32),
                pltpu.SMEM((SCENARIOS, RELEASES), jnp.int32),
                pltpu.SMEM((3, RELEASES), jnp.float32),
                dma((tiles,)),
                dma,
                dma((tiles, 3)),
                dma((tiles, 3)),
                dma((tiles, 4, 2)),
                dma((tiles, 4, 2)),
                dma((scen_count - 1,)),
                dma((scen_count - 1,)),
                dma((scen_count - 1,)),
                dma((scen_count - 1,)),
                dma((grid_count - 1,)),
                dma((grid_count - 1,)),
            ],
            compiler_params=pltpu.CompilerParams(
                collective_id=0, has_side_effects=True, vmem_limit_bytes=40 * 1024 * 1024
            ),
        )(value_next, scenario_ids, inflow_table, release_shifts, price)
        return average - mean[0, 0]

    return jax.shard_map(
        on_device,
        mesh=mesh,
        in_specs=(P("grid", "scen", None), P("scen"), P(), P(), P()),
        out_specs=P("grid", "scen", None),
        check_vma=False,
    )
```

```python
import math

import jax
import jax.numpy as jnp
from jax import lax
from jax.experimental import pallas as pl
from jax.experimental.pallas import tpu as pltpu
from jax.sharding import PartitionSpec as P

H = 8
RELEASES = 16
SCENARIOS = 8
LANES = 128
LOG2E = 1.4426950408889634
MESH = pl.DeviceIdType.MESH
NEAR = 8


def kernel(
    dims,
    x_ref,
    id_hbm,
    inflow_hbm,
    release_hbm,
    price_hbm,
    avg_ref,
    mean_ref,
    raw,
    grown,
    own_id,
    all_ids,
    part_a,
    got_a,
    part_b,
    got_b,
    part_c,
    got_c,
    ids_s,
    id_ref,
    inflow_ref,
    release_ref,
    price_ref,
    base_s,
    amount_s,
    turn_s,
    rate_s,
    local_sem,
    small_sem,
    id_local_sem,
    send_c,
    recv_c,
    send_a,
    recv_a,
    send_id,
    recv_id,
    send_ma,
    recv_ma,
    send_mb,
    recv_mb,
    send_mc,
    recv_mc,
):
    scen_count, grid_count, rows, depth, width = dims
    tiles = width // LANES
    total_rows = rows * grid_count
    total_depth = depth * scen_count
    span = 4 * depth
    reach = rows + 2 * H
    tile_rows = reach * span
    s = lax.axis_index("scen")
    g = lax.axis_index("grid")

    def scen_peer(step):
        return {"scen": lax.rem(s + step + scen_count, scen_count), "grid": g}

    def grid_peer(step):
        return {"scen": s, "grid": lax.rem(g + step + grid_count, grid_count)}

    near = lax.rem(g, NEAR)

    def near_peer(step):
        return {"scen": s, "grid": g - near + lax.rem(near + step, NEAR)}


    def lanes(i):
        return pl.ds(pl.multiple_of(i * LANES, LANES), LANES)

    def own_copy(i):
        return pltpu.make_async_copy(
            x_ref.at[:, :, lanes(i)], raw.at[i, 1, pl.ds(H, rows)], local_sem.at[i]
        )

    def block_copy(i, source, slot, step, use):
        return pltpu.make_async_remote_copy(
            src_ref=x_ref.at[:, :, lanes(i)] if source == 1 else raw.at[i, source, pl.ds(H, rows)],
            dst_ref=raw.at[i, slot, pl.ds(H, rows)],
            send_sem=send_c.at[i, use],
            recv_sem=recv_c.at[i, slot],
            device_id=scen_peer(step),
            device_id_type=MESH,
        )

    def two_back(i):
        return block_copy(i, 1, 3, -2, 0)

    def up(i):
        return block_copy(i, 1, 0, 1, 1)

    def down(i):
        return block_copy(i, 1, 2, -1, 1)

    def relay_up(i):
        return block_copy(i, 2, 0, 2, 2)

    def relay_down(i):
        return block_copy(i, 0, 2, -2, 2)

    def relay_across(i):
        return block_copy(i, 3, 2, 1, 3)

    def landed(i, slot):
        return block_copy(i, 1, slot, -2, 0)

    def grid_copy(i, slot, way):
        if way == 0:
            first, landing, step = 0, H + rows, -1
        else:
            first, landing, step = rows - H, 0, 1
        if slot == 1:
            source = x_ref.at[pl.ds(first, H), :, lanes(i)]
        else:
            source = raw.at[i, slot, pl.ds(H + first, H)]
        return pltpu.make_async_remote_copy(
            src_ref=source,
            dst_ref=raw.at[i, slot, pl.ds(landing, H)],
            send_sem=send_a.at[i, slot, way],
            recv_sem=recv_a.at[i, slot, way],
            device_id=grid_peer(step),
            device_id_type=MESH,
        )

    def halo_copy(i, which, way):
        step, slot = ((1, 0), (-1, 2), (-2, 3))[which]
        landing = H + rows if way == 0 else 0
        return pltpu.make_async_remote_copy(
            src_ref=raw.at[i, 1, pl.ds(landing, H)],
            dst_ref=raw.at[i, slot, pl.ds(landing, H)],
            send_sem=send_a.at[i, slot, 1 - way],
            recv_sem=recv_a.at[i, slot, way],
            device_id=scen_peer(step),
            device_id_type=MESH,
        )

    def id_copy(step):
        return pltpu.make_async_remote_copy(
            src_ref=own_id,
            dst_ref=all_ids.at[s],
            send_sem=send_id.at[step - 1],
            recv_sem=recv_id.at[step - 1],
            device_id=scen_peer(step),
            device_id_type=MESH,
        )

    def mean_a_copy(step):
        return pltpu.make_async_remote_copy(
            src_ref=part_a,
            dst_ref=got_a.at[step - 1],
            send_sem=send_ma.at[step - 1],
            recv_sem=recv_ma.at[step - 1],
            device_id=scen_peer(step),
            device_id_type=MESH,
        )

    def mean_b_copy(step):
        return pltpu.make_async_remote_copy(
            src_ref=part_b,
            dst_ref=got_b.at[step - 1],
            send_sem=send_mb.at[step - 1],
            recv_sem=recv_mb.at[step - 1],
            device_id=near_peer(step),
            device_id_type=MESH,
        )

    def mean_c_copy(step):
        return pltpu.make_async_remote_copy(
            src_ref=part_c,
            dst_ref=got_c.at[step - 1],
            send_sem=send_mc.at[step - 1],
            recv_sem=recv_mc.at[step - 1],
            device_id=grid_peer(step * NEAR),
            device_id_type=MESH,
        )

    def loop(start, stop, body):
        def step(i, carry):
            body(i)
            return carry

        lax.fori_loop(start, stop, step, 0)

    barrier = pltpu.get_barrier_semaphore()

    def greet(peer):
        pl.semaphore_signal(barrier, inc=1, device_id=peer, device_id_type=MESH)

    far_count = grid_count // NEAR
    for step in range(1, scen_count):
        greet(scen_peer(step))
    for step in range(1, NEAR):
        greet(near_peer(step))
    for step in range(1, far_count):
        greet(grid_peer(step * NEAR))
    for step in (-1, 1):
        greet(grid_peer(step))
    small = [
        pltpu.make_async_copy(source, target, small_sem.at[n])
        for n, (source, target) in enumerate(
            ((id_hbm, id_ref), (inflow_hbm, inflow_ref), (release_hbm, release_ref), (price_hbm, price_ref))
        )
    ]
    for copy in small:
        copy.start()
    for i in range(tiles):
        own_copy(i).start()
    for copy in small:
        copy.wait()
    own_id[...] = jnp.full((1, LANES), id_ref[0], jnp.int32)
    all_ids[s] = jnp.full((1, LANES), id_ref[0], jnp.int32)
    pl.semaphore_wait(barrier, scen_count + NEAR + far_count - 1)

    even = lax.rem(s, 2) == 0
    odd = jnp.logical_not(even)
    crosses = (near == 0, near == NEAR - 1)

    def start_all(i):
        for way in (0, 1):
            grid_copy(i, 1, way).start()

        @pl.when(even)
        def _():
            up(i).start()

        @pl.when(odd)
        def _():
            down(i).start()

        two_back(i).start()

    def pass_on(i, slot):
        for way in (0, 1):

            @pl.when(jnp.logical_not(crosses[way]))
            def _():
                grid_copy(i, slot, way).start()

    def by_x(i):
        return lax.rem(i, 4) != 3

    def forward_first(i):
        @pl.when(even)
        def _():
            landed(i, 2).wait_recv()
            relay_up(i).start()
            pass_on(i, 2)

        @pl.when(odd)
        def _():
            landed(i, 0).wait_recv()

            @pl.when(by_x(i))
            def _():
                relay_down(i).start()

            pass_on(i, 0)

        landed(i, 3).wait_recv()

        @pl.when(jnp.logical_and(even, jnp.logical_not(by_x(i))))
        def _():
            relay_across(i).start()

        pass_on(i, 3)
        for way in (0, 1):
            grid_copy(i, 1, way).wait_recv()

            @pl.when(crosses[1 - way])
            def _():
                for which in (0, 1, 2):
                    halo_copy(i, which, way).start()

    def forward_second(i):
        @pl.when(even)
        def _():
            landed(i, 0).wait_recv()
            pass_on(i, 0)

        @pl.when(odd)
        def _():
            landed(i, 2).wait_recv()
            pass_on(i, 2)

    ahead = 3
    for i in range(ahead):
        start_all(i)
    for step in range(1, scen_count):
        id_copy(step).start()
    forward_first(0)

    scale = -LOG2E / 4.0

    def rates(r):
        rate_s[0 * RELEASES + r] = (price_ref[0] * scale / total_rows) * (H - release_ref[0, r]).astype(jnp.float32)
        rate_s[1 * RELEASES + r] = (price_ref[1] * scale / width) * (H - release_ref[1, r]).astype(jnp.float32)
        rate_s[2 * RELEASES + r] = (price_ref[2] * scale / total_depth) * (H - release_ref[2, r]).astype(jnp.float32)

    loop(0, RELEASES, rates)

    for step in range(1, scen_count):
        id_copy(step).wait_recv()
    to_scalar = pltpu.make_async_copy(all_ids, ids_s, id_local_sem)
    to_scalar.start()
    to_scalar.wait()

    def shifts(w):
        row = ids_s[w, 0, 0]
        i1 = inflow_ref[0, row]
        i2 = inflow_ref[1, row]
        i3 = inflow_ref[2, row]

        def one(r):
            u1 = release_ref[0, r]
            u2 = release_ref[1, r]
            u3 = release_ref[2, r]
            along = i2 + u1 - u2
            back = jnp.where(along < 0, 1, 0)
            at = r * SCENARIOS + w
            amount = along + back * LANES
            base_s[at] = (1 - back) * tile_rows + (H + i1 - u1) * span + (depth + i3 + u2 - u3)
            amount_s[at] = amount
            turn_s[at] = jnp.bitwise_and(LANES - amount, LANES - 1)

        loop(0, RELEASES, one)

    loop(0, scen_count, shifts)

    lane = lax.broadcasted_iota(jnp.int32, (depth, LANES), 1)
    level_c = (lax.broadcasted_iota(jnp.int32, (depth, LANES), 0) + s * depth + 1).astype(jnp.float32)
    level_b = (lane + 1).astype(jnp.float32)
    lowest = jnp.where(g == 0, H, 0)
    highest = jnp.where(g == grid_count - 1, H + rows - 1, reach - 1)
    at_first = s == 0
    at_last = s == scen_count - 1
    near_last = s >= scen_count - 2

    def grow(v):
        return jnp.exp2(v * (-2.0 * LOG2E))

    def build(i):
        def some_rows(block):
            for k in range(4):
                a = block * 4 + k
                source = jnp.clip(a, lowest, highest)
                v0 = raw[i, 0, source]
                v1 = raw[i, 1, source]
                v2 = raw[i, 2, source]
                v3 = raw[i, 3, source]
                v0 = jnp.where(at_first, jnp.broadcast_to(v1[0:1], v0.shape), v0)
                v2 = jnp.where(at_last, jnp.broadcast_to(v1[depth - 1 : depth], v0.shape), v2)
                v3 = jnp.where(near_last, jnp.broadcast_to(v2[depth - 1 : depth], v0.shape), v3)
                at = (i + 1) * tile_rows + a * span
                for slot, v in enumerate((v0, v1, v2, v3)):
                    grown[pl.ds(pl.multiple_of(at + slot * depth, depth), depth), :] = grow(v)

        loop(0, reach // 4, some_rows)

    def edge(from_tile, to_tile, column):
        def some(block):
            for k in range(16):
                at = pl.multiple_of((block * 16 + k) * depth, depth)
                v = grown[pl.ds(from_tile * tile_rows + at, depth), :]
                grown[pl.ds(to_tile * tile_rows + at, depth), :] = jnp.broadcast_to(
                    v[:, column : column + 1], (depth, LANES)
                )

        loop(0, tile_rows // depth // 16, some)

    group = 4

    def compute(j, total):
        level = level_b + (j * LANES).astype(jnp.float32)

        def one_group(q, total):
            first = q * group
            offset = j * tile_rows + first * span

            def one_release(r, sums):
                sums = list(sums)
                flat = rate_s[2 * RELEASES + r] * level_c + rate_s[1 * RELEASES + r] * level
                weights = []
                for k in range(group):
                    row = (g * rows + first + k + 1).astype(jnp.float32)
                    weights.append(jnp.exp2(flat + rate_s[0 * RELEASES + r] * row))
                for w in range(SCENARIOS):
                    at = base_s[r * SCENARIOS + w] + offset
                    mask = lane < amount_s[r * SCENARIOS + w]
                    turn = turn_s[r * SCENARIOS + w]
                    for k in range(group):
                        low = grown[pl.ds(at + k * span, depth), :]
                        high = grown[pl.ds(at + k * span + tile_rows, depth), :]
                        landed = pltpu.roll(jnp.where(mask, high, low), turn, 1)
                        sums[w * group + k] = sums[w * group + k] + weights[k] * landed
                return tuple(sums)

            zero = jnp.zeros((depth, LANES), jnp.float32)
            sums = (zero,) * (SCENARIOS * group)
            for r in range(RELEASES):
                sums = one_release(r, sums)
            for k in range(group):
                t = [sums[w * group + k] for w in range(SCENARIOS)]
                logs = jnp.log(t[0] * t[1] * (t[2] * t[3])) + jnp.log(t[4] * t[5] * (t[6] * t[7]))
                row = (g * rows + first + k + 1).astype(jnp.float32)
                top = (
                    (price_ref[2] / total_depth) * level_c
                    + (price_ref[1] / width) * level
                    + (price_ref[0] / total_rows) * row
                )
                value = -top - (0.5 / SCENARIOS) * logs
                avg_ref[first + k, :, lanes(j)] = value
                total = total + value
            return total

        return lax.fori_loop(0, rows // group, one_group, total)

    def finish(i):
        own_copy(i).wait()
        for slot in (0, 2, 3):
            for way in (0, 1):
                grid_copy(i, slot, way).wait_recv()
        build(i)

    def step(i, total):
        @pl.when(i + ahead - 1 < tiles)
        def _():
            start_all(i + ahead - 1)

        @pl.when(i < tiles)
        def _():
            forward_first(i)

        forward_second(i - 1)
        total = lax.cond(i >= 3, lambda t: compute(i - 3, t), lambda t: t, total)
        finish(i - 1)

        @pl.when(i == 1)
        def _():
            edge(1, 0, 0)

        return total

    total = jnp.zeros((depth, LANES), jnp.float32)
    total = lax.fori_loop(1, tiles + 1, step, total)
    edge(tiles, tiles + 1, LANES - 1)
    total = lax.fori_loop(tiles - 2, tiles, compute, total)

    def drain(i):
        two_back(i).wait_send()
        up(i).wait_send()

        @pl.when(jnp.logical_or(even, by_x(i)))
        def _():
            relay_up(i).wait_send()

        @pl.when(jnp.logical_and(even, jnp.logical_not(by_x(i))))
        def _():
            relay_across(i).wait_send()

        for slot in range(4):
            for way in (0, 1):
                grid_copy(i, slot, way).wait_send()

    part_a[...] = jnp.sum(total, axis=0, keepdims=True)
    for step in range(1, scen_count):
        mean_a_copy(step).start()
    for step in range(1, scen_count):
        id_copy(step).wait_send()
    loop(0, tiles, drain)
    for step in range(1, scen_count):
        mean_a_copy(step).wait_recv()
    part_b[...] = part_a[...] + jnp.sum(got_a[...], axis=0)
    for step in range(1, NEAR):
        mean_b_copy(step).start()
    for step in range(1, NEAR):
        mean_b_copy(step).wait_recv()
    part_c[...] = part_b[...] + jnp.sum(got_b[...], axis=0)
    for step in range(1, far_count):
        mean_c_copy(step).start()
    for step in range(1, far_count):
        mean_c_copy(step).wait_recv()
    whole = part_c[...] + jnp.sum(got_c[...], axis=0)
    cells = float(total_rows * total_depth * width)
    mean_ref[...] = jnp.broadcast_to(jnp.sum(whole, axis=1, keepdims=True) / cells, (1, LANES))
    for step in range(1, scen_count):
        mean_a_copy(step).wait_send()
    for step in range(1, NEAR):
        mean_b_copy(step).wait_send()
    for step in range(1, far_count):
        mean_c_copy(step).wait_send()


def solution(mesh):
    scen_count = mesh.shape["scen"]
    grid_count = mesh.shape["grid"]

    def on_device(value_next, scenario_ids, inflow_table, release_shifts, price):
        rows, depth, width = value_next.shape
        tiles = width // LANES
        dims = (scen_count, grid_count, rows, depth, width)
        reach = rows + 2 * H
        vmem = pl.BlockSpec(memory_space=pltpu.VMEM)
        dma = pltpu.SemaphoreType.DMA
        average, mean = pl.pallas_call(
            lambda *refs: kernel(dims, *refs),
            out_shape=(
                jax.ShapeDtypeStruct((rows, depth, width), jnp.float32),
                jax.ShapeDtypeStruct((1, LANES), jnp.float32),
            ),
            in_specs=[pl.BlockSpec(memory_space=pl.ANY)] * 5,
            out_specs=(vmem, vmem),
            scratch_shapes=[
                pltpu.VMEM((tiles, 4, reach, depth, LANES), jnp.float32),
                pltpu.VMEM(((tiles + 2) * reach * 4 * depth, LANES), jnp.float32),
                pltpu.VMEM((1, LANES), jnp.int32),
                pltpu.VMEM((scen_count, 1, LANES), jnp.int32),
                pltpu.VMEM((1, LANES), jnp.float32),
                pltpu.VMEM((scen_count - 1, 1, LANES), jnp.float32),
                pltpu.VMEM((1, LANES), jnp.float32),
                pltpu.VMEM((NEAR - 1, 1, LANES), jnp.float32),
                pltpu.VMEM((1, LANES), jnp.float32),
                pltpu.VMEM((grid_count // NEAR - 1, 1, LANES), jnp.float32),
                pltpu.SMEM((scen_count, 1, LANES), jnp.int32),
                pltpu.SMEM(scenario_ids.shape, jnp.int32),
                pltpu.SMEM(inflow_table.shape[::-1], jnp.int32),
                pltpu.SMEM(release_shifts.shape[::-1], jnp.int32),
                pltpu.SMEM(price.shape, jnp.float32),
                pltpu.SMEM((SCENARIOS * RELEASES,), jnp.int32),
                pltpu.SMEM((SCENARIOS * RELEASES,), jnp.int32),
                pltpu.SMEM((SCENARIOS * RELEASES,), jnp.int32),
                pltpu.SMEM((3 * RELEASES,), jnp.float32),
                dma((tiles,)),
                dma((4,)),
                dma,
                dma((tiles, 4)),
                dma((tiles, 4)),
                dma((tiles, 4, 2)),
                dma((tiles, 4, 2)),
                dma((scen_count - 1,)),
                dma((scen_count - 1,)),
                dma((scen_count - 1,)),
                dma((scen_count - 1,)),
                dma((NEAR - 1,)),
                dma((NEAR - 1,)),
                dma((grid_count // NEAR - 1,)),
                dma((grid_count // NEAR - 1,)),
            ],
            compiler_params=pltpu.CompilerParams(
                collective_id=0, has_side_effects=True, vmem_limit_bytes=40 * 1024 * 1024
            ),
        )(value_next, scenario_ids, inflow_table.T, release_shifts.T, price)
        return average - mean[0, 0]

    return jax.shard_map(
        on_device,
        mesh=mesh,
        in_specs=(P("grid", "scen", None), P("scen"), P(), P(), P()),
        out_specs=P("grid", "scen", None),
        check_vma=False,
    )
```

```python
import math

import jax
import jax.numpy as jnp
from jax import lax
from jax.experimental import pallas as pl
from jax.experimental.pallas import tpu as pltpu
from jax.sharding import PartitionSpec as P

H = 8
RELEASES = 16
SCENARIOS = 8
LANES = 128
LOG2E = 1.4426950408889634
MESH = pl.DeviceIdType.MESH
NEAR = 8


def kernel(
    dims,
    x_ref,
    id_hbm,
    inflow_hbm,
    release_hbm,
    price_hbm,
    avg_ref,
    mean_ref,
    held,
    packed,
    raw,
    side,
    grown,
    outgoing,
    result,
    own_id,
    all_ids,
    part_a,
    got_a,
    part_b,
    got_b,
    part_c,
    got_c,
    ids_s,
    id_ref,
    inflow_ref,
    release_ref,
    price_ref,
    base_s,
    other_s,
    amount_s,
    turn_s,
    rate_s,
    held_sem,
    local_sem,
    small_sem,
    send_x,
    recv_x,
    send_y,
    recv_y,
    send_a,
    recv_a,
    send_b,
    recv_b,
    send_o,
    recv_o,
    send_id,
    recv_id,
    send_ma,
    recv_ma,
    send_mb,
    recv_mb,
    send_mc,
    recv_mc,
):
    scen_count, grid_count, rows, depth, width = dims
    total_rows = rows * grid_count
    total_depth = depth * scen_count
    span = total_depth + 3 * depth
    reach = rows + 2 * H
    tile_rows = reach * span
    pack = 4
    s = lax.axis_index("scen")
    g = lax.axis_index("grid")
    near = lax.rem(g, NEAR)
    far_count = grid_count // NEAR

    def scen_index(step):
        return lax.rem(s + step + scen_count, scen_count)

    def scen_peer(step):
        return {"scen": scen_index(step), "grid": g}

    def grid_peer(step):
        return {"scen": s, "grid": lax.rem(g + step + grid_count, grid_count)}

    def near_peer(step):
        return {"scen": s, "grid": g - near + lax.rem(near + step, NEAR)}

    def lanes(i):
        return pl.ds(pl.multiple_of(i * LANES, LANES), LANES)

    def remote(source, target, send_sem, recv_sem, peer):
        return pltpu.make_async_remote_copy(
            src_ref=source,
            dst_ref=target,
            send_sem=send_sem,
            recv_sem=recv_sem,
            device_id=peer,
            device_id_type=MESH,
        )

    def tile_copy(step):
        return remote(
            x_ref.at[:, :, lanes(scen_index(step))],
            raw.at[s, pl.ds(H, rows)],
            send_x.at[step - 1],
            recv_x.at[step - 1],
            scen_peer(step),
        )

    def side_copy(step):
        return remote(
            packed.at[scen_index(step)],
            side.at[s, pl.ds(H // pack, rows // pack)],
            send_y.at[step - 1],
            recv_y.at[step - 1],
            scen_peer(step),
        )

    def row_copy(step, way):
        q = scen_index(-step)
        first, landing, to = ((H, H + rows, -1), (rows, 0, 1))[way]
        return remote(
            raw.at[q, pl.ds(first, H)],
            raw.at[q, pl.ds(landing, H)],
            send_a.at[step, way],
            recv_a.at[step, way],
            grid_peer(to),
        )

    def row_side_copy(step, way):
        q = scen_index(-step)
        first, landing, to = ((H, H + rows, -1), (rows, 0, 1))[way]
        return remote(
            side.at[q, pl.ds(first // pack, H // pack)],
            side.at[q, pl.ds(landing // pack, H // pack)],
            send_b.at[step, way],
            recv_b.at[step, way],
            grid_peer(to),
        )

    def out_copy(step):
        return remote(
            outgoing.at[scen_index(step)],
            result.at[s],
            send_o.at[step - 1],
            recv_o.at[step - 1],
            scen_peer(step),
        )

    def id_copy(step):
        return remote(
            own_id, all_ids.at[s], send_id.at[step - 1], recv_id.at[step - 1], scen_peer(step)
        )

    def mean_a_copy(step):
        return remote(
            part_a, got_a.at[step - 1], send_ma.at[step - 1], recv_ma.at[step - 1], scen_peer(step)
        )

    def mean_b_copy(step):
        return remote(
            part_b, got_b.at[step - 1], send_mb.at[step - 1], recv_mb.at[step - 1], near_peer(step)
        )

    def mean_c_copy(step):
        return remote(
            part_c,
            got_c.at[step - 1],
            send_mc.at[step - 1],
            recv_mc.at[step - 1],
            grid_peer(step * NEAR),
        )

    def loop(start, stop, body):
        def step(i, carry):
            body(i)
            return carry

        lax.fori_loop(start, stop, step, 0)

    barrier = pltpu.get_barrier_semaphore()

    def greet(peer):
        pl.semaphore_signal(barrier, inc=1, device_id=peer, device_id_type=MESH)

    for step in range(1, scen_count):
        greet(scen_peer(step))
    for step in range(1, NEAR):
        greet(near_peer(step))
    for step in range(1, far_count):
        greet(grid_peer(step * NEAR))
    for step in (-1, 1):
        greet(grid_peer(step))

    to_held = pltpu.make_async_copy(x_ref, held, held_sem)
    to_held.start()
    small = [
        pltpu.make_async_copy(source, target, small_sem.at[n])
        for n, (source, target) in enumerate(
            ((id_hbm, id_ref), (inflow_hbm, inflow_ref), (release_hbm, release_ref), (price_hbm, price_ref))
        )
    ]
    for copy in small:
        copy.start()
    own_tile = pltpu.make_async_copy(
        x_ref.at[:, :, lanes(s)], raw.at[s, pl.ds(H, rows)], local_sem.at[0]
    )
    own_tile.start()
    for copy in small:
        copy.wait()
    own_id[...] = jnp.full((1, LANES), id_ref[0], jnp.int32)
    all_ids[s] = jnp.full((1, LANES), id_ref[0], jnp.int32)

    lane = lax.broadcasted_iota(jnp.int32, (depth, LANES), 1)
    to_held.wait()

    def pack_group(p):
        for k in range(scen_count):
            together = None
            for r in range(pack):
                a = p * pack + r
                if k > 0:
                    before = held[a, :, (k - 1) * LANES : k * LANES]
                else:
                    before = jnp.broadcast_to(held[a, :, 0:LANES][:, 0:1], (depth, LANES))
                if k < scen_count - 1:
                    after = held[a, :, (k + 1) * LANES : (k + 2) * LANES]
                else:
                    last = held[a, :, k * LANES : (k + 1) * LANES]
                    after = jnp.broadcast_to(last[:, LANES - 1 : LANES], (depth, LANES))
                both = jnp.where(lane < LANES // 2, after, before)
                if r == 0:
                    together = both
                else:
                    mine = jnp.bitwise_and(lane - 32 * r + H, LANES - 1) < 3 * H
                    together = jnp.where(mine, pltpu.roll(both, 32 * r, 1), together)
            packed[k, p] = together

    loop(0, rows // pack, pack_group)
    own_side = pltpu.make_async_copy(
        packed.at[s], side.at[s, pl.ds(H // pack, rows // pack)], local_sem.at[1]
    )
    own_side.start()

    pl.semaphore_wait(barrier, scen_count + NEAR + far_count - 1)
    order = (4, 3, 5, 2, 6, 1, 7)
    for step in order:
        tile_copy(step).start()
        side_copy(step).start()
    for step in range(1, scen_count):
        id_copy(step).start()

    def pass_rows(step):
        for way in (0, 1):
            row_copy(step, way).start()
            row_side_copy(step, way).start()

    own_tile.wait()
    own_side.wait()
    pass_rows(0)

    scale = -LOG2E / 4.0

    def rates(r):
        rate_s[r] = (price_ref[0] * scale / total_rows) * (H - release_ref[0, r]).astype(jnp.float32)
        rate_s[RELEASES + r] = (price_ref[1] * scale / width) * (H - release_ref[1, r]).astype(jnp.float32)
        rate_s[2 * RELEASES + r] = (price_ref[2] * scale / total_depth) * (H - release_ref[2, r]).astype(
            jnp.float32
        )

    loop(0, RELEASES, rates)

    for step in range(1, scen_count):
        id_copy(step).wait_recv()
    to_scalar = pltpu.make_async_copy(all_ids, ids_s, local_sem.at[2])
    to_scalar.start()
    to_scalar.wait()

    def shifts(w):
        row = ids_s[w, 0, 0]
        i1 = inflow_ref[0, row]
        i2 = inflow_ref[1, row]
        i3 = inflow_ref[2, row]

        def one(r):
            u1 = release_ref[0, r]
            u2 = release_ref[1, r]
            u3 = release_ref[2, r]
            along = i2 + u1 - u2
            back = jnp.where(along < 0, 1, 0)
            at = r * SCENARIOS + w
            amount = along + back * LANES
            base_s[at] = back * tile_rows + (H + i1 - u1) * span + (depth + i3 + u2 - u3)
            other_s[at] = (1 - back) * tile_rows + (H + i1 - u1) * span + (depth + i3 + u2 - u3)
            amount_s[at] = amount
            turn_s[at] = jnp.bitwise_and(LANES - amount, LANES - 1)

        loop(0, RELEASES, one)

    loop(0, scen_count, shifts)

    for step in order:
        tile_copy(step).wait_recv()
        side_copy(step).wait_recv()
        pass_rows(step)

    lowest = jnp.where(g == 0, H, 0)
    highest = jnp.where(g == grid_count - 1, H + rows - 1, reach - 1)

    def grow(v):
        return jnp.exp2(v * (-2.0 * LOG2E))

    def build(q):
        def some_rows(block):
            for k in range(4):
                a = block * 4 + k
                source = jnp.clip(a, lowest, highest)
                at = pl.multiple_of(a * span + (q + 1) * depth, depth)
                grown[pl.ds(at, depth), :] = grow(raw[q, source])
                turned = jnp.bitwise_and(LANES - 32 * lax.rem(source, pack), LANES - 1)
                grown[pl.ds(tile_rows + at, depth), :] = grow(
                    pltpu.roll(side[q, source // pack], turned, 1)
                )

        loop(0, reach // 4, some_rows)

    def build_step(step):
        for way in (0, 1):
            row_copy(step, way).wait_recv()
            row_side_copy(step, way).wait_recv()
        build(scen_index(-step))

    build_step(0)
    for step in order:
        build_step(step)

    def outer(block):
        for k in range(4):
            row = (block * 4 + k) * span
            low = grown[pl.ds(pl.multiple_of(row + depth, depth), depth), :]
            high = grown[pl.ds(pl.multiple_of(row + total_depth, depth), depth), :]
            grown[pl.ds(pl.multiple_of(row, depth), depth), :] = jnp.broadcast_to(low[0:1], low.shape)
            top = jnp.broadcast_to(high[depth - 1 : depth], low.shape)
            for extra in (1, 2):
                at = pl.multiple_of(row + total_depth + extra * depth, depth)
                grown[pl.ds(at, depth), :] = top

    loop(0, 2 * reach // 4, outer)

    group = 4
    level_b = (lane + s * LANES + 1).astype(jnp.float32)
    level_in = lax.broadcasted_iota(jnp.int32, (depth, LANES), 0) + 1

    def compute(q, step, total):
        t = scen_index(step)
        first = q * group
        offset = t * depth + first * span
        level_c = (level_in + t * depth).astype(jnp.float32)
        sums = [jnp.zeros((depth, LANES), jnp.float32)] * (SCENARIOS * group)
        for r in range(RELEASES):
            flat = rate_s[2 * RELEASES + r] * level_c + rate_s[RELEASES + r] * level_b
            weights = []
            for k in range(group):
                row = (g * rows + first + k + 1).astype(jnp.float32)
                weights.append(jnp.exp2(flat + rate_s[r] * row))
            for w in range(SCENARIOS):
                at = base_s[r * SCENARIOS + w] + offset
                other = other_s[r * SCENARIOS + w] + offset
                mask = lane < amount_s[r * SCENARIOS + w]
                turn = turn_s[r * SCENARIOS + w]
                for k in range(group):
                    low = grown[pl.ds(at + k * span, depth), :]
                    high = grown[pl.ds(other + k * span, depth), :]
                    landed = pltpu.roll(jnp.where(mask, high, low), turn, 1)
                    sums[w * group + k] = sums[w * group + k] + weights[k] * landed
        for k in range(group):
            v = [sums[w * group + k] for w in range(SCENARIOS)]
            logs = jnp.log(v[0] * v[1] * (v[2] * v[3])) + jnp.log(v[4] * v[5] * (v[6] * v[7]))
            row = (g * rows + first + k + 1).astype(jnp.float32)
            top = (
                (price_ref[2] / total_depth) * level_c
                + (price_ref[1] / width) * level_b
                + (price_ref[0] / total_rows) * row
            )
            value = -top - (0.5 / SCENARIOS) * logs
            outgoing[t, first + k] = value
            total = total + value
        return total

    def part(n, total):
        step = 1 + n // (rows // group)
        q = lax.rem(n, rows // group)

        @pl.when(jnp.logical_and(q == 1, step >= 2))
        def _():
            out_copy(step - 1).start()

        return compute(q, step, total)

    total = jnp.zeros((depth, LANES), jnp.float32)
    total = lax.fori_loop(0, scen_count * (rows // group), part, total)

    part_a[...] = jnp.sum(total, axis=0, keepdims=True)
    for step in range(1, scen_count):
        mean_a_copy(step).start()
    for step in range(1, scen_count):
        id_copy(step).wait_send()
        tile_copy(step).wait_send()
        side_copy(step).wait_send()
    for step in range(scen_count):
        for way in (0, 1):
            row_copy(step, way).wait_send()
            row_side_copy(step, way).wait_send()
    for step in range(1, scen_count):
        mean_a_copy(step).wait_recv()
    part_b[...] = part_a[...] + jnp.sum(got_a[...], axis=0)
    for step in range(1, NEAR):
        mean_b_copy(step).start()
    result[s] = outgoing[s]
    for step in range(1, scen_count):
        out_copy(step).wait_recv()
        out_copy(step).wait_send()
    for k in range(scen_count):
        avg_ref[:, :, k * LANES : (k + 1) * LANES] = result[k]
    for step in range(1, NEAR):
        mean_b_copy(step).wait_recv()
    part_c[...] = part_b[...] + jnp.sum(got_b[...], axis=0)
    for step in range(1, far_count):
        mean_c_copy(step).start()
    for step in range(1, scen_count):
        mean_a_copy(step).wait_send()
    for step in range(1, NEAR):
        mean_b_copy(step).wait_send()
    for step in range(1, far_count):
        mean_c_copy(step).wait_recv()
    whole = part_c[...] + jnp.sum(got_c[...], axis=0)
    cells = float(total_rows * total_depth * width)
    mean_ref[...] = jnp.broadcast_to(jnp.sum(whole, axis=1, keepdims=True) / cells, (1, LANES))
    for step in range(1, far_count):
        mean_c_copy(step).wait_send()


def solution(mesh):
    scen_count = mesh.shape["scen"]
    grid_count = mesh.shape["grid"]

    def on_device(value_next, scenario_ids, inflow_table, release_shifts, price):
        rows, depth, width = value_next.shape
        dims = (scen_count, grid_count, rows, depth, width)
        reach = rows + 2 * H
        span = depth * (scen_count + 3)
        far_count = grid_count // NEAR
        vmem = pl.BlockSpec(memory_space=pltpu.VMEM)
        dma = pltpu.SemaphoreType.DMA
        peers = scen_count - 1
        f32, i32 = jnp.float32, jnp.int32
        average, mean = pl.pallas_call(
            lambda *refs: kernel(dims, *refs),
            out_shape=(
                jax.ShapeDtypeStruct((rows, depth, width), f32),
                jax.ShapeDtypeStruct((1, LANES), f32),
            ),
            in_specs=[pl.BlockSpec(memory_space=pl.ANY)] * 5,
            out_specs=(vmem, vmem),
            scratch_shapes=[
                pltpu.VMEM((rows, depth, width), f32),
                pltpu.VMEM((scen_count, rows // 4, depth, LANES), f32),
                pltpu.VMEM((scen_count, reach, depth, LANES), f32),
                pltpu.VMEM((scen_count, reach // 4, depth, LANES), f32),
                pltpu.VMEM((2 * reach * span, LANES), f32),
                pltpu.VMEM((scen_count, rows, depth, LANES), f32),
                pltpu.VMEM((scen_count, rows, depth, LANES), f32),
                pltpu.VMEM((1, LANES), i32),
                pltpu.VMEM((scen_count, 1, LANES), i32),
                pltpu.VMEM((1, LANES), f32),
                pltpu.VMEM((peers, 1, LANES), f32),
                pltpu.VMEM((1, LANES), f32),
                pltpu.VMEM((NEAR - 1, 1, LANES), f32),
                pltpu.VMEM((1, LANES), f32),
                pltpu.VMEM((far_count - 1, 1, LANES), f32),
                pltpu.SMEM((scen_count, 1, LANES), i32),
                pltpu.SMEM(scenario_ids.shape, i32),
                pltpu.SMEM(inflow_table.shape[::-1], i32),
                pltpu.SMEM(release_shifts.shape[::-1], i32),
                pltpu.SMEM(price.shape, f32),
                pltpu.SMEM((SCENARIOS * RELEASES,), i32),
                pltpu.SMEM((SCENARIOS * RELEASES,), i32),
                pltpu.SMEM((SCENARIOS * RELEASES,), i32),
                pltpu.SMEM((SCENARIOS * RELEASES,), i32),
                pltpu.SMEM((3 * RELEASES,), f32),
                dma,
                dma((3,)),
                dma((4,)),
                dma((peers,)),
                dma((peers,)),
                dma((peers,)),
                dma((peers,)),
                dma((scen_count, 2)),
                dma((scen_count, 2)),
                dma((scen_count, 2)),
                dma((scen_count, 2)),
                dma((peers,)),
                dma((peers,)),
                dma((peers,)),
                dma((peers,)),
                dma((peers,)),
                dma((peers,)),
                dma((NEAR - 1,)),
                dma((NEAR - 1,)),
                dma((far_count - 1,)),
                dma((far_count - 1,)),
            ],
            compiler_params=pltpu.CompilerParams(
                collective_id=0, has_side_effects=True, vmem_limit_bytes=60 * 1024 * 1024
            ),
        )(value_next, scenario_ids, inflow_table.T, release_shifts.T, price)
        return average - mean[0, 0]

    return jax.shard_map(
        on_device,
        mesh=mesh,
        in_specs=(P("grid", "scen", None), P("scen"), P(), P(), P()),
        out_specs=P("grid", "scen", None),
        check_vma=False,
    )
```

```python
import math

import jax
import jax.numpy as jnp
from jax import lax
from jax.experimental import pallas as pl
from jax.experimental.pallas import tpu as pltpu
from jax.sharding import PartitionSpec as P

H = 8
RELEASES = 16
SCENARIOS = 8
LANES = 128
LOG2E = 1.4426950408889634
MESH = pl.DeviceIdType.MESH
NEAR = 8


def kernel(
    dims,
    x_ref,
    id_hbm,
    inflow_hbm,
    release_hbm,
    price_hbm,
    avg_ref,
    mean_ref,
    held,
    packed,
    raw,
    side,
    grown,
    outgoing,
    result,
    own_id,
    all_ids,
    part_a,
    got_a,
    part_b,
    got_b,
    part_c,
    got_c,
    ids_s,
    id_ref,
    inflow_ref,
    release_ref,
    price_ref,
    base_s,
    other_s,
    amount_s,
    turn_s,
    rate_s,
    held_sem,
    local_sem,
    small_sem,
    send_x,
    recv_x,
    send_y,
    recv_y,
    send_a,
    recv_a,
    send_b,
    recv_b,
    send_o,
    recv_o,
    send_id,
    recv_id,
    send_ma,
    recv_ma,
    send_mb,
    recv_mb,
    send_mc,
    recv_mc,
):
    scen_count, grid_count, rows, depth, width = dims
    total_rows = rows * grid_count
    total_depth = depth * scen_count
    span = total_depth + 3 * depth
    reach = rows + 2 * H
    tile_rows = reach * span
    pack = 4
    s = lax.axis_index("scen")
    g = lax.axis_index("grid")
    near = lax.rem(g, NEAR)
    far_count = grid_count // NEAR

    def scen_index(step):
        return lax.rem(s + step + scen_count, scen_count)

    def scen_peer(step):
        return {"scen": scen_index(step), "grid": g}

    def grid_peer(step):
        return {"scen": s, "grid": lax.rem(g + step + grid_count, grid_count)}

    def near_peer(step):
        return {"scen": s, "grid": g - near + lax.rem(near + step, NEAR)}

    def lanes(i):
        return pl.ds(pl.multiple_of(i * LANES, LANES), LANES)

    def remote(source, target, send_sem, recv_sem, peer):
        return pltpu.make_async_remote_copy(
            src_ref=source,
            dst_ref=target,
            send_sem=send_sem,
            recv_sem=recv_sem,
            device_id=peer,
            device_id_type=MESH,
        )

    def tile_copy(step):
        return remote(
            x_ref.at[:, :, lanes(scen_index(step))],
            raw.at[s, pl.ds(H, rows)],
            send_x.at[step - 1],
            recv_x.at[step - 1],
            scen_peer(step),
        )

    def side_copy(step):
        return remote(
            packed.at[scen_index(step)],
            side.at[s, pl.ds(H // pack, rows // pack)],
            send_y.at[step - 1],
            recv_y.at[step - 1],
            scen_peer(step),
        )

    def row_copy(step, way):
        q = scen_index(-step)
        first, landing, to = ((H, H + rows, -1), (rows, 0, 1))[way]
        return remote(
            raw.at[q, pl.ds(first, H)],
            raw.at[q, pl.ds(landing, H)],
            send_a.at[step, way],
            recv_a.at[step, way],
            grid_peer(to),
        )

    def row_side_copy(step, way):
        q = scen_index(-step)
        first, landing, to = ((H, H + rows, -1), (rows, 0, 1))[way]
        return remote(
            side.at[q, pl.ds(first // pack, H // pack)],
            side.at[q, pl.ds(landing // pack, H // pack)],
            send_b.at[step, way],
            recv_b.at[step, way],
            grid_peer(to),
        )

    def out_copy(step):
        return remote(
            outgoing.at[scen_index(step)],
            result.at[s],
            send_o.at[step - 1],
            recv_o.at[step - 1],
            scen_peer(step),
        )

    def id_copy(step):
        return remote(
            own_id, all_ids.at[s], send_id.at[step - 1], recv_id.at[step - 1], scen_peer(step)
        )

    def mean_a_copy(step):
        return remote(
            part_a, got_a.at[step - 1], send_ma.at[step - 1], recv_ma.at[step - 1], scen_peer(step)
        )

    def mean_b_copy(step):
        return remote(
            part_b, got_b.at[step - 1], send_mb.at[step - 1], recv_mb.at[step - 1], near_peer(step)
        )

    def mean_c_copy(step):
        return remote(
            part_c,
            got_c.at[step - 1],
            send_mc.at[step - 1],
            recv_mc.at[step - 1],
            grid_peer(step * NEAR),
        )

    def loop(start, stop, body):
        def step(i, carry):
            body(i)
            return carry

        lax.fori_loop(start, stop, step, 0)

    barrier = pltpu.get_barrier_semaphore()

    def greet(peer):
        pl.semaphore_signal(barrier, inc=1, device_id=peer, device_id_type=MESH)

    for step in range(1, scen_count):
        greet(scen_peer(step))
    for step in range(1, NEAR):
        greet(near_peer(step))
    for step in range(1, far_count):
        greet(grid_peer(step * NEAR))
    for step in (-1, 1):
        greet(grid_peer(step))

    to_held = pltpu.make_async_copy(x_ref, held, held_sem)
    to_held.start()
    small = [
        pltpu.make_async_copy(source, target, small_sem.at[n])
        for n, (source, target) in enumerate(
            ((id_hbm, id_ref), (inflow_hbm, inflow_ref), (release_hbm, release_ref), (price_hbm, price_ref))
        )
    ]
    for copy in small:
        copy.start()
    own_tile = pltpu.make_async_copy(
        x_ref.at[:, :, lanes(s)], raw.at[s, pl.ds(H, rows)], local_sem.at[0]
    )
    own_tile.start()
    for copy in small:
        copy.wait()
    own_id[...] = jnp.full((1, LANES), id_ref[0], jnp.int32)
    all_ids[s] = jnp.full((1, LANES), id_ref[0], jnp.int32)

    lane = lax.broadcasted_iota(jnp.int32, (depth, LANES), 1)
    to_held.wait()

    def pack_group(p):
        for k in range(scen_count):
            together = None
            for r in range(pack):
                a = p * pack + r
                if k > 0:
                    before = held[a, :, (k - 1) * LANES : k * LANES]
                else:
                    before = jnp.broadcast_to(held[a, :, 0:LANES][:, 0:1], (depth, LANES))
                if k < scen_count - 1:
                    after = held[a, :, (k + 1) * LANES : (k + 2) * LANES]
                else:
                    last = held[a, :, k * LANES : (k + 1) * LANES]
                    after = jnp.broadcast_to(last[:, LANES - 1 : LANES], (depth, LANES))
                both = jnp.where(lane < LANES // 2, after, before)
                if r == 0:
                    together = both
                else:
                    mine = jnp.bitwise_and(lane - 32 * r + H, LANES - 1) < 3 * H
                    together = jnp.where(mine, pltpu.roll(both, 32 * r, 1), together)
            packed[k, p] = together

    loop(0, rows // pack, pack_group)
    own_side = pltpu.make_async_copy(
        packed.at[s], side.at[s, pl.ds(H // pack, rows // pack)], local_sem.at[1]
    )
    own_side.start()

    pl.semaphore_wait(barrier, scen_count + NEAR + far_count - 1)
    order = (1, 7, 6, 5, 4, 3, 2)
    for step in order:
        tile_copy(step).start()
        side_copy(step).start()
    for step in range(1, scen_count):
        id_copy(step).start()

    def pass_rows(step):
        for way in (0, 1):
            row_copy(step, way).start()
            row_side_copy(step, way).start()

    own_tile.wait()
    own_side.wait()
    pass_rows(0)

    def take(step):
        tile_copy(step).wait_recv()
        side_copy(step).wait_recv()
        pass_rows(step)

    early = 3
    for step in order[:early]:
        take(step)

    scale = -LOG2E / 4.0

    def rates(r):
        rate_s[r] = (price_ref[0] * scale / total_rows) * (H - release_ref[0, r]).astype(jnp.float32)
        rate_s[RELEASES + r] = (price_ref[1] * scale / width) * (H - release_ref[1, r]).astype(jnp.float32)
        rate_s[2 * RELEASES + r] = (price_ref[2] * scale / total_depth) * (H - release_ref[2, r]).astype(
            jnp.float32
        )

    loop(0, RELEASES, rates)

    for step in range(1, scen_count):
        id_copy(step).wait_recv()
    to_scalar = pltpu.make_async_copy(all_ids, ids_s, local_sem.at[2])
    to_scalar.start()
    to_scalar.wait()

    def shifts(w):
        row = ids_s[w, 0, 0]
        i1 = inflow_ref[0, row]
        i2 = inflow_ref[1, row]
        i3 = inflow_ref[2, row]

        def one(r):
            u1 = release_ref[0, r]
            u2 = release_ref[1, r]
            u3 = release_ref[2, r]
            along = i2 + u1 - u2
            back = jnp.where(along < 0, 1, 0)
            at = r * SCENARIOS + w
            amount = along + back * LANES
            base_s[at] = back * tile_rows + (H + i1 - u1) * span + (depth + i3 + u2 - u3)
            other_s[at] = (1 - back) * tile_rows + (H + i1 - u1) * span + (depth + i3 + u2 - u3)
            amount_s[at] = amount
            turn_s[at] = jnp.bitwise_and(LANES - amount, LANES - 1)

        loop(0, RELEASES, one)

    loop(0, scen_count, shifts)

    for step in order[early:]:
        take(step)

    lowest = jnp.where(g == 0, H, 0)
    highest = jnp.where(g == grid_count - 1, H + rows - 1, reach - 1)

    def grow(v):
        return jnp.exp2(v * (-2.0 * LOG2E))

    def build(q):
        def some_rows(block):
            for k in range(4):
                a = block * 4 + k
                source = jnp.clip(a, lowest, highest)
                at = pl.multiple_of(a * span + (q + 1) * depth, depth)
                grown[pl.ds(at, depth), :] = grow(raw[q, source])
                turned = jnp.bitwise_and(LANES - 32 * lax.rem(source, pack), LANES - 1)
                grown[pl.ds(tile_rows + at, depth), :] = grow(
                    pltpu.roll(side[q, source // pack], turned, 1)
                )

        loop(0, reach // 4, some_rows)

        @pl.when(q == 0)
        def _():
            def below(block):
                for k in range(8):
                    row = (block * 8 + k) * span
                    low = grown[pl.ds(pl.multiple_of(row + depth, depth), depth), :]
                    grown[pl.ds(pl.multiple_of(row, depth), depth), :] = jnp.broadcast_to(
                        low[0:1], low.shape
                    )

            loop(0, 2 * reach // 8, below)

        @pl.when(q == scen_count - 1)
        def _():
            def above(block):
                for k in range(8):
                    row = (block * 8 + k) * span
                    high = grown[pl.ds(pl.multiple_of(row + total_depth, depth), depth), :]
                    top = jnp.broadcast_to(high[depth - 1 : depth], high.shape)
                    for extra in (1, 2):
                        at = pl.multiple_of(row + total_depth + extra * depth, depth)
                        grown[pl.ds(at, depth), :] = top

            loop(0, 2 * reach // 8, above)

    def build_step(step):
        for way in (0, 1):
            row_copy(step, way).wait_recv()
            row_side_copy(step, way).wait_recv()
        build(scen_index(-step))

    loop(0, 2, build_step)
    loop(scen_count - 2, scen_count, build_step)

    group = 4
    level_b = (lane + s * LANES + 1).astype(jnp.float32)
    level_in = lax.broadcasted_iota(jnp.int32, (depth, LANES), 0) + 1

    def compute(q, step, total):
        t = scen_index(step)
        first = q * group
        offset = t * depth + first * span
        level_c = (level_in + t * depth).astype(jnp.float32)
        sums = [jnp.zeros((depth, LANES), jnp.float32)] * (SCENARIOS * group)
        for r in range(RELEASES):
            flat = rate_s[2 * RELEASES + r] * level_c + rate_s[RELEASES + r] * level_b
            weights = []
            for k in range(group):
                row = (g * rows + first + k + 1).astype(jnp.float32)
                weights.append(jnp.exp2(flat + rate_s[r] * row))
            for w in range(SCENARIOS):
                at = base_s[r * SCENARIOS + w] + offset
                other = other_s[r * SCENARIOS + w] + offset
                mask = lane < amount_s[r * SCENARIOS + w]
                turn = turn_s[r * SCENARIOS + w]
                for k in range(group):
                    low = grown[pl.ds(at + k * span, depth), :]
                    high = grown[pl.ds(other + k * span, depth), :]
                    landed = pltpu.roll(jnp.where(mask, high, low), turn, 1)
                    sums[w * group + k] = sums[w * group + k] + weights[k] * landed
        for k in range(group):
            v = [sums[w * group + k] for w in range(SCENARIOS)]
            logs = jnp.log(v[0] * v[1] * (v[2] * v[3])) + jnp.log(v[4] * v[5] * (v[6] * v[7]))
            row = (g * rows + first + k + 1).astype(jnp.float32)
            top = (
                (price_ref[2] / total_depth) * level_c
                + (price_ref[1] / width) * level_b
                + (price_ref[0] / total_rows) * row
            )
            value = -top - (0.5 / SCENARIOS) * logs
            outgoing[t, first + k] = value
            total = total + value
        return total

    def part(n, total):
        step = n // (rows // group)
        q = lax.rem(n, rows // group)

        @pl.when(jnp.logical_and(q == 0, jnp.logical_and(step >= 1, step <= scen_count - 4)))
        def _():
            build_step(scen_count - 2 - step)

        @pl.when(jnp.logical_and(q == 1, step >= 2))
        def _():
            out_copy(step - 1).start()

        return compute(q, step, total)

    total = jnp.zeros((depth, LANES), jnp.float32)
    total = lax.fori_loop(0, scen_count * (rows // group), part, total)

    part_a[...] = jnp.sum(total, axis=0, keepdims=True)
    for step in range(1, scen_count):
        mean_a_copy(step).start()
    out_copy(scen_count - 1).start()
    for step in range(1, scen_count):
        id_copy(step).wait_send()
        tile_copy(step).wait_send()
        side_copy(step).wait_send()
    for step in range(scen_count):
        for way in (0, 1):
            row_copy(step, way).wait_send()
            row_side_copy(step, way).wait_send()
    for step in range(1, scen_count):
        mean_a_copy(step).wait_recv()
    part_b[...] = part_a[...] + jnp.sum(got_a[...], axis=0)
    for step in range(1, NEAR):
        mean_b_copy(step).start()
    result[s] = outgoing[s]
    for step in range(1, scen_count):
        out_copy(step).wait_recv()
        out_copy(step).wait_send()
    for k in range(scen_count):
        avg_ref[:, :, k * LANES : (k + 1) * LANES] = result[k]
    for step in range(1, NEAR):
        mean_b_copy(step).wait_recv()
    part_c[...] = part_b[...] + jnp.sum(got_b[...], axis=0)
    for step in range(1, far_count):
        mean_c_copy(step).start()
    for step in range(1, scen_count):
        mean_a_copy(step).wait_send()
    for step in range(1, NEAR):
        mean_b_copy(step).wait_send()
    for step in range(1, far_count):
        mean_c_copy(step).wait_recv()
    whole = part_c[...] + jnp.sum(got_c[...], axis=0)
    cells = float(total_rows * total_depth * width)
    mean_ref[...] = jnp.broadcast_to(jnp.sum(whole, axis=1, keepdims=True) / cells, (1, LANES))
    for step in range(1, far_count):
        mean_c_copy(step).wait_send()


def solution(mesh):
    scen_count = mesh.shape["scen"]
    grid_count = mesh.shape["grid"]

    def on_device(value_next, scenario_ids, inflow_table, release_shifts, price):
        rows, depth, width = value_next.shape
        dims = (scen_count, grid_count, rows, depth, width)
        reach = rows + 2 * H
        span = depth * (scen_count + 3)
        far_count = grid_count // NEAR
        vmem = pl.BlockSpec(memory_space=pltpu.VMEM)
        dma = pltpu.SemaphoreType.DMA
        peers = scen_count - 1
        f32, i32 = jnp.float32, jnp.int32
        average, mean = pl.pallas_call(
            lambda *refs: kernel(dims, *refs),
            out_shape=(
                jax.ShapeDtypeStruct((rows, depth, width), f32),
                jax.ShapeDtypeStruct((1, LANES), f32),
            ),
            in_specs=[pl.BlockSpec(memory_space=pltpu.HBM)] * 5,
            out_specs=(vmem, vmem),
            scratch_shapes=[
                pltpu.VMEM((rows, depth, width), f32),
                pltpu.VMEM((scen_count, rows // 4, depth, LANES), f32),
                pltpu.VMEM((scen_count, reach, depth, LANES), f32),
                pltpu.VMEM((scen_count, reach // 4, depth, LANES), f32),
                pltpu.VMEM((2 * reach * span, LANES), f32),
                pltpu.VMEM((scen_count, rows, depth, LANES), f32),
                pltpu.VMEM((scen_count, rows, depth, LANES), f32),
                pltpu.VMEM((1, LANES), i32),
                pltpu.VMEM((scen_count, 1, LANES), i32),
                pltpu.VMEM((1, LANES), f32),
                pltpu.VMEM((peers, 1, LANES), f32),
                pltpu.VMEM((1, LANES), f32),
                pltpu.VMEM((NEAR - 1, 1, LANES), f32),
                pltpu.VMEM((1, LANES), f32),
                pltpu.VMEM((far_count - 1, 1, LANES), f32),
                pltpu.SMEM((scen_count, 1, LANES), i32),
                pltpu.SMEM(scenario_ids.shape, i32),
                pltpu.SMEM(inflow_table.shape[::-1], i32),
                pltpu.SMEM(release_shifts.shape[::-1], i32),
                pltpu.SMEM(price.shape, f32),
                pltpu.SMEM((SCENARIOS * RELEASES,), i32),
                pltpu.SMEM((SCENARIOS * RELEASES,), i32),
                pltpu.SMEM((SCENARIOS * RELEASES,), i32),
                pltpu.SMEM((SCENARIOS * RELEASES,), i32),
                pltpu.SMEM((3 * RELEASES,), f32),
                dma,
                dma((3,)),
                dma((4,)),
                dma((peers,)),
                dma((peers,)),
                dma((peers,)),
                dma((peers,)),
                dma((scen_count, 2)),
                dma((scen_count, 2)),
                dma((scen_count, 2)),
                dma((scen_count, 2)),
                dma((peers,)),
                dma((peers,)),
                dma((peers,)),
                dma((peers,)),
                dma((peers,)),
                dma((peers,)),
                dma((NEAR - 1,)),
                dma((NEAR - 1,)),
                dma((far_count - 1,)),
                dma((far_count - 1,)),
            ],
            compiler_params=pltpu.CompilerParams(
                collective_id=0, has_side_effects=True, vmem_limit_bytes=24 * 1024 * 1024
            ),
        )(value_next, scenario_ids, inflow_table.T, release_shifts.T, price)
        return average - mean[0, 0]

    return jax.shard_map(
        on_device,
        mesh=mesh,
        in_specs=(P("grid", "scen", None), P("scen"), P(), P(), P()),
        out_specs=P("grid", "scen", None),
        check_vma=False,
    )
```

```python
import math

import jax
import jax.numpy as jnp
from jax import lax
from jax.experimental import pallas as pl
from jax.experimental.pallas import tpu as pltpu
from jax.sharding import PartitionSpec as P

H = 8
SHIFTS = 3 * H + 1
RELEASES = 16
SCENARIOS = 8
LANES = 128
LOG2E = 1.4426950408889634
MESH = pl.DeviceIdType.MESH
NEAR = 8


def kernel(
    dims,
    x_ref,
    id_hbm,
    inflow_hbm,
    release_hbm,
    price_hbm,
    avg_ref,
    mean_ref,
    held,
    packed,
    raw,
    side,
    grown,
    outgoing,
    result,
    own_id,
    all_ids,
    part_a,
    got_a,
    part_b,
    got_b,
    part_c,
    got_c,
    ids_s,
    id_ref,
    inflow_ref,
    release_ref,
    price_ref,
    base_s,
    rate_s,
    held_sem,
    local_sem,
    small_sem,
    send_x,
    recv_x,
    send_y,
    recv_y,
    send_a,
    recv_a,
    send_b,
    recv_b,
    send_o,
    recv_o,
    send_id,
    recv_id,
    send_ma,
    recv_ma,
    send_mb,
    recv_mb,
    send_mc,
    recv_mc,
):
    scen_count, grid_count, rows, depth, width = dims
    total_rows = rows * grid_count
    total_depth = depth * scen_count
    span = total_depth + 3 * depth
    reach = rows + 2 * H
    tile_rows = reach * span
    pack = 4
    s = lax.axis_index("scen")
    g = lax.axis_index("grid")
    near = lax.rem(g, NEAR)
    far_count = grid_count // NEAR

    def scen_index(step):
        return lax.rem(s + step + scen_count, scen_count)

    def scen_peer(step):
        return {"scen": scen_index(step), "grid": g}

    def grid_peer(step):
        return {"scen": s, "grid": lax.rem(g + step + grid_count, grid_count)}

    def near_peer(step):
        return {"scen": s, "grid": g - near + lax.rem(near + step, NEAR)}

    def lanes(i):
        return pl.ds(pl.multiple_of(i * LANES, LANES), LANES)

    def remote(source, target, send_sem, recv_sem, peer):
        return pltpu.make_async_remote_copy(
            src_ref=source,
            dst_ref=target,
            send_sem=send_sem,
            recv_sem=recv_sem,
            device_id=peer,
            device_id_type=MESH,
        )

    def tile_copy(step):
        return remote(
            x_ref.at[:, :, lanes(scen_index(step))],
            raw.at[s, pl.ds(H, rows)],
            send_x.at[step - 1],
            recv_x.at[step - 1],
            scen_peer(step),
        )

    def side_copy(step):
        return remote(
            packed.at[scen_index(step)],
            side.at[s, pl.ds(H // pack, rows // pack)],
            send_y.at[step - 1],
            recv_y.at[step - 1],
            scen_peer(step),
        )

    def row_copy(step, way):
        q = scen_index(-step)
        first, landing, to = ((H, H + rows, -1), (rows, 0, 1))[way]
        return remote(
            raw.at[q, pl.ds(first, H)],
            raw.at[q, pl.ds(landing, H)],
            send_a.at[step, way],
            recv_a.at[step, way],
            grid_peer(to),
        )

    def row_side_copy(step, way):
        q = scen_index(-step)
        first, landing, to = ((H, H + rows, -1), (rows, 0, 1))[way]
        return remote(
            side.at[q, pl.ds(first // pack, H // pack)],
            side.at[q, pl.ds(landing // pack, H // pack)],
            send_b.at[step, way],
            recv_b.at[step, way],
            grid_peer(to),
        )

    def out_copy(step):
        return remote(
            outgoing.at[scen_index(step)],
            result.at[s],
            send_o.at[step - 1],
            recv_o.at[step - 1],
            scen_peer(step),
        )

    def id_copy(step):
        return remote(
            own_id, all_ids.at[s], send_id.at[step - 1], recv_id.at[step - 1], scen_peer(step)
        )

    def mean_a_copy(step):
        return remote(
            part_a, got_a.at[step - 1], send_ma.at[step - 1], recv_ma.at[step - 1], scen_peer(step)
        )

    def mean_b_copy(step):
        return remote(
            part_b, got_b.at[step - 1], send_mb.at[step - 1], recv_mb.at[step - 1], near_peer(step)
        )

    def mean_c_copy(step):
        return remote(
            part_c,
            got_c.at[step - 1],
            send_mc.at[step - 1],
            recv_mc.at[step - 1],
            grid_peer(step * NEAR),
        )

    def loop(start, stop, body):
        def step(i, carry):
            body(i)
            return carry

        lax.fori_loop(start, stop, step, 0)

    barrier = pltpu.get_barrier_semaphore()

    def greet(peer):
        pl.semaphore_signal(barrier, inc=1, device_id=peer, device_id_type=MESH)

    for step in range(1, scen_count):
        greet(scen_peer(step))
    for step in range(1, NEAR):
        greet(near_peer(step))
    for step in range(1, far_count):
        greet(grid_peer(step * NEAR))
    for step in (-1, 1):
        greet(grid_peer(step))

    to_held = pltpu.make_async_copy(x_ref, held, held_sem)
    to_held.start()
    small = [
        pltpu.make_async_copy(source, target, small_sem.at[n])
        for n, (source, target) in enumerate(
            ((id_hbm, id_ref), (inflow_hbm, inflow_ref), (release_hbm, release_ref), (price_hbm, price_ref))
        )
    ]
    for copy in small:
        copy.start()
    own_tile = pltpu.make_async_copy(
        x_ref.at[:, :, lanes(s)], raw.at[s, pl.ds(H, rows)], local_sem.at[0]
    )
    own_tile.start()
    for copy in small:
        copy.wait()
    own_id[...] = jnp.full((1, LANES), id_ref[0], jnp.int32)
    all_ids[s] = jnp.full((1, LANES), id_ref[0], jnp.int32)

    lane = lax.broadcasted_iota(jnp.int32, (depth, LANES), 1)
    to_held.wait()

    def pack_group(p):
        for k in range(scen_count):
            together = None
            for r in range(pack):
                a = p * pack + r
                if k > 0:
                    before = held[a, :, (k - 1) * LANES : k * LANES]
                else:
                    before = jnp.broadcast_to(held[a, :, 0:LANES][:, 0:1], (depth, LANES))
                if k < scen_count - 1:
                    after = held[a, :, (k + 1) * LANES : (k + 2) * LANES]
                else:
                    last = held[a, :, k * LANES : (k + 1) * LANES]
                    after = jnp.broadcast_to(last[:, LANES - 1 : LANES], (depth, LANES))
                both = jnp.where(lane < LANES // 2, after, before)
                if r == 0:
                    together = both
                else:
                    mine = jnp.bitwise_and(lane - 32 * r + H, LANES - 1) < 3 * H
                    together = jnp.where(mine, pltpu.roll(both, 32 * r, 1), together)
            packed[k, p] = together

    loop(0, rows // pack, pack_group)
    own_side = pltpu.make_async_copy(
        packed.at[s], side.at[s, pl.ds(H // pack, rows // pack)], local_sem.at[1]
    )
    own_side.start()

    pl.semaphore_wait(barrier, scen_count + NEAR + far_count - 1)
    order = (1, 7, 6, 5, 4, 3, 2)
    for step in order:
        tile_copy(step).start()
        side_copy(step).start()
    for step in range(1, scen_count):
        id_copy(step).start()

    def pass_rows(step):
        for way in (0, 1):
            row_copy(step, way).start()
            row_side_copy(step, way).start()

    own_tile.wait()
    own_side.wait()
    pass_rows(0)

    def take(step):
        tile_copy(step).wait_recv()
        side_copy(step).wait_recv()
        pass_rows(step)

    early = 3
    for step in order[:early]:
        take(step)

    scale = -LOG2E / 4.0

    def rates(r):
        rate_s[r] = (price_ref[0] * scale / total_rows) * (H - release_ref[0, r]).astype(jnp.float32)
        rate_s[RELEASES + r] = (price_ref[1] * scale / width) * (H - release_ref[1, r]).astype(jnp.float32)
        rate_s[2 * RELEASES + r] = (price_ref[2] * scale / total_depth) * (H - release_ref[2, r]).astype(
            jnp.float32
        )

    loop(0, RELEASES, rates)

    for step in range(1, scen_count):
        id_copy(step).wait_recv()
    to_scalar = pltpu.make_async_copy(all_ids, ids_s, local_sem.at[2])
    to_scalar.start()
    to_scalar.wait()

    def shifts(w):
        row = ids_s[w, 0, 0]
        i1 = inflow_ref[0, row]
        i2 = inflow_ref[1, row]
        i3 = inflow_ref[2, row]

        def one(r):
            u1 = release_ref[0, r]
            u2 = release_ref[1, r]
            u3 = release_ref[2, r]
            copy = H + i2 + u1 - u2
            base_s[r * SCENARIOS + w] = (
                copy * tile_rows + (H + i1 - u1) * span + (depth + i3 + u2 - u3)
            )

        loop(0, RELEASES, one)

    loop(0, scen_count, shifts)


    lowest = jnp.where(g == 0, H, 0)
    highest = jnp.where(g == grid_count - 1, H + rows - 1, reach - 1)

    def grow(v):
        return jnp.exp2(v * (-2.0 * LOG2E))

    def build(q):
        def some_rows(block):
            for k in range(4):
                a = block * 4 + k
                source = jnp.clip(a, lowest, highest)
                at = pl.multiple_of(a * span + (q + 1) * depth, depth)
                main = grow(raw[q, source])
                turned = jnp.bitwise_and(LANES - 32 * lax.rem(source, pack), LANES - 1)
                beside = grow(pltpu.roll(side[q, source // pack], turned, 1))
                for copy in range(SHIFTS):
                    shift = copy - H
                    if shift == 0:
                        moved = main
                    elif shift > 0:
                        moved = pltpu.roll(jnp.where(lane < shift, beside, main), LANES - shift, 1)
                    else:
                        moved = pltpu.roll(
                            jnp.where(lane >= LANES + shift, beside, main), -shift, 1
                        )
                    grown[pl.ds(copy * tile_rows + at, depth), :] = moved

        loop(0, reach // 4, some_rows)

        @pl.when(q == 0)
        def _():
            def below(block):
                for k in range(8):
                    row = (block * 8 + k) * span
                    low = grown[pl.ds(pl.multiple_of(row + depth, depth), 1), :]
                    grown[pl.ds(pl.multiple_of(row, depth), depth), :] = jnp.broadcast_to(
                        low, (depth, LANES)
                    )

            loop(0, SHIFTS * reach // 8, below)

        @pl.when(q == scen_count - 1)
        def _():
            def above(block):
                for k in range(8):
                    row = (block * 8 + k) * span
                    high = grown[pl.ds(row + total_depth + depth - 1, 1), :]
                    top = jnp.broadcast_to(high, (depth, LANES))
                    for extra in (1, 2):
                        at = pl.multiple_of(row + total_depth + extra * depth, depth)
                        grown[pl.ds(at, depth), :] = top

            loop(0, SHIFTS * reach // 8, above)

    def build_step(step):
        for way in (0, 1):
            row_copy(step, way).wait_recv()
            row_side_copy(step, way).wait_recv()
        build(scen_index(-step))

    build_step(0)
    for n, step in enumerate(order[early:]):
        take(step)
        if n < early:
            build_step(order[n])

    group = 4
    level_b = (lane + s * LANES + 1).astype(jnp.float32)
    level_in = lax.broadcasted_iota(jnp.int32, (depth, LANES), 0) + 1

    def compute(q, step, total):
        t = scen_index(step)
        first = q * group
        offset = t * depth + first * span
        level_c = (level_in + t * depth).astype(jnp.float32)
        def one_release(r, sums):
            sums = list(sums)
            flat = rate_s[2 * RELEASES + r] * level_c + rate_s[RELEASES + r] * level_b
            weights = []
            for k in range(group):
                row = (g * rows + first + k + 1).astype(jnp.float32)
                weights.append(jnp.exp2(flat + rate_s[r] * row))
            for w in range(SCENARIOS):
                at = base_s[r * SCENARIOS + w] + offset
                for k in range(group):
                    landed = grown[pl.ds(at + k * span, depth), :]
                    sums[w * group + k] = sums[w * group + k] + weights[k] * landed
            return tuple(sums)

        sums = lax.fori_loop(
            0, RELEASES, one_release, (jnp.zeros((depth, LANES), jnp.float32),) * (SCENARIOS * group), unroll=4
        )
        for k in range(group):
            v = [sums[w * group + k] for w in range(SCENARIOS)]
            logs = jnp.log(v[0] * v[1] * (v[2] * v[3])) + jnp.log(v[4] * v[5] * (v[6] * v[7]))
            row = (g * rows + first + k + 1).astype(jnp.float32)
            top = (
                (price_ref[2] / total_depth) * level_c
                + (price_ref[1] / width) * level_b
                + (price_ref[0] / total_rows) * row
            )
            value = -top - (0.5 / SCENARIOS) * logs
            outgoing[t, first + k] = value
            total = total + value
        return total

    def part(n, total):
        step = n // (rows // group)
        q = lax.rem(n, rows // group)

        @pl.when(jnp.logical_and(q == 0, jnp.logical_and(step >= 1, step <= scen_count - 4)))
        def _():
            build_step(scen_count - 2 - step)

        @pl.when(jnp.logical_and(q == 1, step >= 2))
        def _():
            out_copy(step - 1).start()

        return compute(q, step, total)

    total = jnp.zeros((depth, LANES), jnp.float32)
    total = lax.fori_loop(0, scen_count * (rows // group), part, total)

    part_a[...] = jnp.sum(total, axis=0, keepdims=True)
    for step in range(1, scen_count):
        mean_a_copy(step).start()
    out_copy(scen_count - 1).start()
    for step in range(1, scen_count):
        id_copy(step).wait_send()
        tile_copy(step).wait_send()
        side_copy(step).wait_send()
    for step in range(scen_count):
        for way in (0, 1):
            row_copy(step, way).wait_send()
            row_side_copy(step, way).wait_send()
    for step in range(1, scen_count):
        mean_a_copy(step).wait_recv()
    part_b[...] = part_a[...] + jnp.sum(got_a[...], axis=0)
    for step in range(1, NEAR):
        mean_b_copy(step).start()
    result[s] = outgoing[s]
    for step in range(1, scen_count):
        out_copy(step).wait_recv()
        out_copy(step).wait_send()
    for k in range(scen_count):
        avg_ref[:, :, k * LANES : (k + 1) * LANES] = result[k]
    for step in range(1, NEAR):
        mean_b_copy(step).wait_recv()
    part_c[...] = part_b[...] + jnp.sum(got_b[...], axis=0)
    for step in range(1, far_count):
        mean_c_copy(step).start()
    for step in range(1, scen_count):
        mean_a_copy(step).wait_send()
    for step in range(1, NEAR):
        mean_b_copy(step).wait_send()
    for step in range(1, far_count):
        mean_c_copy(step).wait_recv()
    whole = part_c[...] + jnp.sum(got_c[...], axis=0)
    cells = float(total_rows * total_depth * width)
    mean_ref[...] = jnp.broadcast_to(jnp.sum(whole, axis=1, keepdims=True) / cells, (1, LANES))
    for step in range(1, far_count):
        mean_c_copy(step).wait_send()


def solution(mesh):
    scen_count = mesh.shape["scen"]
    grid_count = mesh.shape["grid"]

    def on_device(value_next, scenario_ids, inflow_table, release_shifts, price):
        rows, depth, width = value_next.shape
        dims = (scen_count, grid_count, rows, depth, width)
        reach = rows + 2 * H
        span = depth * (scen_count + 3)
        far_count = grid_count // NEAR
        vmem = pl.BlockSpec(memory_space=pltpu.VMEM)
        dma = pltpu.SemaphoreType.DMA
        peers = scen_count - 1
        f32, i32 = jnp.float32, jnp.int32
        average, mean = pl.pallas_call(
            lambda *refs: kernel(dims, *refs),
            out_shape=(
                jax.ShapeDtypeStruct((rows, depth, width), f32),
                jax.ShapeDtypeStruct((1, LANES), f32),
            ),
            in_specs=[pl.BlockSpec(memory_space=pltpu.HBM)] * 5,
            out_specs=(vmem, vmem),
            scratch_shapes=[
                pltpu.VMEM((rows, depth, width), f32),
                pltpu.VMEM((scen_count, rows // 4, depth, LANES), f32),
                pltpu.VMEM((scen_count, reach, depth, LANES), f32),
                pltpu.VMEM((scen_count, reach // 4, depth, LANES), f32),
                pltpu.VMEM((SHIFTS * reach * span, LANES), f32),
                pltpu.VMEM((scen_count, rows, depth, LANES), f32),
                pltpu.VMEM((scen_count, rows, depth, LANES), f32),
                pltpu.VMEM((1, LANES), i32),
                pltpu.VMEM((scen_count, 1, LANES), i32),
                pltpu.VMEM((1, LANES), f32),
                pltpu.VMEM((peers, 1, LANES), f32),
                pltpu.VMEM((1, LANES), f32),
                pltpu.VMEM((NEAR - 1, 1, LANES), f32),
                pltpu.VMEM((1, LANES), f32),
                pltpu.VMEM((far_count - 1, 1, LANES), f32),
                pltpu.SMEM((scen_count, 1, LANES), i32),
                pltpu.SMEM(scenario_ids.shape, i32),
                pltpu.SMEM(inflow_table.shape[::-1], i32),
                pltpu.SMEM(release_shifts.shape[::-1], i32),
                pltpu.SMEM(price.shape, f32),
                pltpu.SMEM((SCENARIOS * RELEASES,), i32),
                pltpu.SMEM((3 * RELEASES,), f32),
                dma,
                dma((3,)),
                dma((4,)),
                dma((peers,)),
                dma((peers,)),
                dma((peers,)),
                dma((peers,)),
                dma((scen_count, 2)),
                dma((scen_count, 2)),
                dma((scen_count, 2)),
                dma((scen_count, 2)),
                dma((peers,)),
                dma((peers,)),
                dma((peers,)),
                dma((peers,)),
                dma((peers,)),
                dma((peers,)),
                dma((NEAR - 1,)),
                dma((NEAR - 1,)),
                dma((far_count - 1,)),
                dma((far_count - 1,)),
            ],
            compiler_params=pltpu.CompilerParams(
                collective_id=0, has_side_effects=True, vmem_limit_bytes=52 * 1024 * 1024
            ),
        )(value_next, scenario_ids, inflow_table.T, release_shifts.T, price)
        return average - mean[0, 0]

    return jax.shard_map(
        on_device,
        mesh=mesh,
        in_specs=(P("grid", "scen", None), P("scen"), P(), P(), P()),
        out_specs=P("grid", "scen", None),
        check_vma=False,
    )
```

```python
import math

import jax
import jax.numpy as jnp
from jax import lax
from jax.experimental import pallas as pl
from jax.experimental.pallas import tpu as pltpu
from jax.sharding import PartitionSpec as P

H = 8
SHIFTS = 3 * H + 1
RELEASES = 16
SCENARIOS = 8
LANES = 128
LOG2E = 1.4426950408889634
MESH = pl.DeviceIdType.MESH
NEAR = 8


def kernel(
    dims,
    x_ref,
    id_hbm,
    inflow_hbm,
    release_hbm,
    price_hbm,
    avg_ref,
    mean_ref,
    held,
    packed,
    raw,
    side,
    grown,
    outgoing,
    result,
    own_id,
    all_ids,
    part_a,
    got_a,
    part_b,
    got_b,
    part_c,
    got_c,
    ids_s,
    id_ref,
    inflow_ref,
    release_ref,
    price_ref,
    base_s,
    rate_s,
    held_sem,
    local_sem,
    small_sem,
    send_x,
    recv_x,
    send_y,
    recv_y,
    send_a,
    recv_a,
    send_b,
    recv_b,
    send_o,
    recv_o,
    send_id,
    recv_id,
    send_ma,
    recv_ma,
    send_mb,
    recv_mb,
    send_mc,
    recv_mc,
):
    scen_count, grid_count, rows, depth, width = dims
    total_rows = rows * grid_count
    total_depth = depth * scen_count
    span = total_depth + 3 * depth
    reach = rows + 2 * H
    tile_rows = reach * span
    pack = 4
    s = lax.axis_index("scen")
    g = lax.axis_index("grid")
    near = lax.rem(g, NEAR)
    far_count = grid_count // NEAR

    def scen_index(step):
        return lax.rem(s + step + scen_count, scen_count)

    def scen_peer(step):
        return {"scen": scen_index(step), "grid": g}

    def grid_peer(step):
        return {"scen": s, "grid": lax.rem(g + step + grid_count, grid_count)}

    def near_peer(step):
        return {"scen": s, "grid": g - near + lax.rem(near + step, NEAR)}

    def lanes(i):
        return pl.ds(pl.multiple_of(i * LANES, LANES), LANES)

    def remote(source, target, send_sem, recv_sem, peer):
        return pltpu.make_async_remote_copy(
            src_ref=source,
            dst_ref=target,
            send_sem=send_sem,
            recv_sem=recv_sem,
            device_id=peer,
            device_id_type=MESH,
        )

    def tile_copy(step):
        return remote(
            x_ref.at[:, :, lanes(scen_index(step))],
            raw.at[s, pl.ds(H, rows)],
            send_x.at[step - 1],
            recv_x.at[step - 1],
            scen_peer(step),
        )

    def side_copy(step):
        return remote(
            packed.at[scen_index(step)],
            side.at[s, pl.ds(H // pack, rows // pack)],
            send_y.at[step - 1],
            recv_y.at[step - 1],
            scen_peer(step),
        )

    def row_copy(step, way):
        q = scen_index(-step)
        first, landing, to = ((H, H + rows, -1), (rows, 0, 1))[way]
        return remote(
            raw.at[q, pl.ds(first, H)],
            raw.at[q, pl.ds(landing, H)],
            send_a.at[step, way],
            recv_a.at[step, way],
            grid_peer(to),
        )

    def row_side_copy(step, way):
        q = scen_index(-step)
        first, landing, to = ((H, H + rows, -1), (rows, 0, 1))[way]
        return remote(
            side.at[q, pl.ds(first // pack, H // pack)],
            side.at[q, pl.ds(landing // pack, H // pack)],
            send_b.at[step, way],
            recv_b.at[step, way],
            grid_peer(to),
        )

    def out_copy(step):
        return remote(
            outgoing.at[scen_index(step)],
            result.at[s],
            send_o.at[step - 1],
            recv_o.at[step - 1],
            scen_peer(step),
        )

    def id_copy(step):
        return remote(
            own_id, all_ids.at[s], send_id.at[step - 1], recv_id.at[step - 1], scen_peer(step)
        )

    def mean_a_copy(step):
        return remote(
            part_a, got_a.at[step - 1], send_ma.at[step - 1], recv_ma.at[step - 1], scen_peer(step)
        )

    def mean_b_copy(step):
        return remote(
            part_b, got_b.at[step - 1], send_mb.at[step - 1], recv_mb.at[step - 1], near_peer(step)
        )

    def mean_c_copy(step):
        return remote(
            part_c,
            got_c.at[step - 1],
            send_mc.at[step - 1],
            recv_mc.at[step - 1],
            grid_peer(step * NEAR),
        )

    def loop(start, stop, body):
        def step(i, carry):
            body(i)
            return carry

        lax.fori_loop(start, stop, step, 0)

    barrier = pltpu.get_barrier_semaphore()

    def greet(peer):
        pl.semaphore_signal(barrier, inc=1, device_id=peer, device_id_type=MESH)

    for step in range(1, scen_count):
        greet(scen_peer(step))
    for step in range(1, NEAR):
        greet(near_peer(step))
    for step in range(1, far_count):
        greet(grid_peer(step * NEAR))
    for step in (-1, 1):
        greet(grid_peer(step))

    to_held = pltpu.make_async_copy(x_ref, held, held_sem)
    to_held.start()
    small = [
        pltpu.make_async_copy(source, target, small_sem.at[n])
        for n, (source, target) in enumerate(
            ((id_hbm, id_ref), (inflow_hbm, inflow_ref), (release_hbm, release_ref), (price_hbm, price_ref))
        )
    ]
    for copy in small:
        copy.start()
    own_tile = pltpu.make_async_copy(
        x_ref.at[:, :, lanes(s)], raw.at[s, pl.ds(H, rows)], local_sem.at[0]
    )
    own_tile.start()
    for copy in small:
        copy.wait()
    own_id[...] = jnp.full((1, LANES), id_ref[0], jnp.int32)
    all_ids[s] = jnp.full((1, LANES), id_ref[0], jnp.int32)

    lane = lax.broadcasted_iota(jnp.int32, (depth, LANES), 1)
    to_held.wait()

    def pack_group(p):
        for k in range(scen_count):
            together = None
            for r in range(pack):
                a = p * pack + r
                if k > 0:
                    before = held[a, :, (k - 1) * LANES : k * LANES]
                else:
                    before = jnp.broadcast_to(held[a, :, 0:LANES][:, 0:1], (depth, LANES))
                if k < scen_count - 1:
                    after = held[a, :, (k + 1) * LANES : (k + 2) * LANES]
                else:
                    last = held[a, :, k * LANES : (k + 1) * LANES]
                    after = jnp.broadcast_to(last[:, LANES - 1 : LANES], (depth, LANES))
                both = jnp.where(lane < LANES // 2, after, before)
                if r == 0:
                    together = both
                else:
                    mine = jnp.bitwise_and(lane - 32 * r + H, LANES - 1) < 3 * H
                    together = jnp.where(mine, pltpu.roll(both, 32 * r, 1), together)
            packed[k, p] = together

    loop(0, rows // pack, pack_group)
    own_side = pltpu.make_async_copy(
        packed.at[s], side.at[s, pl.ds(H // pack, rows // pack)], local_sem.at[1]
    )
    own_side.start()

    pl.semaphore_wait(barrier, scen_count + NEAR + far_count - 1)
    order = (1, 7, 6, 5, 4, 3, 2)
    for step in order:
        tile_copy(step).start()
        side_copy(step).start()
    for step in range(1, scen_count):
        id_copy(step).start()

    def pass_rows(step):
        for way in (0, 1):
            row_copy(step, way).start()
            row_side_copy(step, way).start()

    own_tile.wait()
    own_side.wait()
    pass_rows(0)

    def take(step):
        tile_copy(step).wait_recv()
        side_copy(step).wait_recv()
        pass_rows(step)

    early = 3
    for step in order[:early]:
        take(step)

    scale = -LOG2E / 4.0

    def rates(r):
        rate_s[r] = (price_ref[0] * scale / total_rows) * (H - release_ref[0, r]).astype(jnp.float32)
        rate_s[RELEASES + r] = (price_ref[1] * scale / width) * (H - release_ref[1, r]).astype(jnp.float32)
        rate_s[2 * RELEASES + r] = (price_ref[2] * scale / total_depth) * (H - release_ref[2, r]).astype(
            jnp.float32
        )

    loop(0, RELEASES, rates)

    for step in range(1, scen_count):
        id_copy(step).wait_recv()
    to_scalar = pltpu.make_async_copy(all_ids, ids_s, local_sem.at[2])
    to_scalar.start()
    to_scalar.wait()

    def shifts(w):
        row = ids_s[w, 0, 0]
        i1 = inflow_ref[0, row]
        i2 = inflow_ref[1, row]
        i3 = inflow_ref[2, row]

        def one(r):
            u1 = release_ref[0, r]
            u2 = release_ref[1, r]
            u3 = release_ref[2, r]
            copy = H + i2 + u1 - u2
            base_s[r * SCENARIOS + w] = (
                copy * tile_rows + (H + i1 - u1) * span + (depth + i3 + u2 - u3)
            )

        loop(0, RELEASES, one)

    loop(0, scen_count, shifts)


    lowest = jnp.where(g == 0, H, 0)
    highest = jnp.where(g == grid_count - 1, H + rows - 1, reach - 1)

    def grow(v):
        return jnp.exp2(v * (-2.0 * LOG2E))

    def build(q):
        def some_rows(block):
            for k in range(4):
                a = block * 4 + k
                source = jnp.clip(a, lowest, highest)
                at = pl.multiple_of(a * span + (q + 1) * depth, depth)
                main = grow(raw[q, source])
                turned = jnp.bitwise_and(LANES - 32 * lax.rem(source, pack), LANES - 1)
                beside = grow(pltpu.roll(side[q, source // pack], turned, 1))
                for copy in range(SHIFTS):
                    shift = copy - H
                    if shift == 0:
                        moved = main
                    elif shift > 0:
                        moved = pltpu.roll(jnp.where(lane < shift, beside, main), LANES - shift, 1)
                    else:
                        moved = pltpu.roll(
                            jnp.where(lane >= LANES + shift, beside, main), -shift, 1
                        )
                    grown[pl.ds(copy * tile_rows + at, depth), :] = moved

        loop(0, reach // 4, some_rows)

        @pl.when(q == 0)
        def _():
            def below(block):
                for k in range(8):
                    row = (block * 8 + k) * span
                    low = grown[pl.ds(pl.multiple_of(row + depth, depth), 1), :]
                    grown[pl.ds(pl.multiple_of(row, depth), depth), :] = jnp.broadcast_to(
                        low, (depth, LANES)
                    )

            loop(0, SHIFTS * reach // 8, below)

        @pl.when(q == scen_count - 1)
        def _():
            def above(block):
                for k in range(8):
                    row = (block * 8 + k) * span
                    high = grown[pl.ds(row + total_depth + depth - 1, 1), :]
                    top = jnp.broadcast_to(high, (depth, LANES))
                    for extra in (1, 2):
                        at = pl.multiple_of(row + total_depth + extra * depth, depth)
                        grown[pl.ds(at, depth), :] = top

            loop(0, SHIFTS * reach // 8, above)

    def build_step(step):
        for way in (0, 1):
            row_copy(step, way).wait_recv()
            row_side_copy(step, way).wait_recv()
        build(scen_index(-step))

    build_step(0)
    for n, step in enumerate(order[early:]):
        take(step)
        if n < early:
            build_step(order[n])

    group = 4
    level_b = (lane + s * LANES + 1).astype(jnp.float32)
    level_in = lax.broadcasted_iota(jnp.int32, (depth, LANES), 0) + 1

    def compute(q, step, total):
        t = scen_index(step)
        first = q * group
        offset = t * depth + first * span
        level_c = (level_in + t * depth).astype(jnp.float32)
        def one_release(r, sums):
            sums = list(sums)
            flat = rate_s[2 * RELEASES + r] * level_c + rate_s[RELEASES + r] * level_b
            weights = []
            for k in range(group):
                row = (g * rows + first + k + 1).astype(jnp.float32)
                weights.append(jnp.exp2(flat + rate_s[r] * row))
            for w in range(SCENARIOS):
                at = base_s[r * SCENARIOS + w] + offset
                for k in range(group):
                    landed = grown[pl.ds(at + k * span, depth), :]
                    sums[w * group + k] = sums[w * group + k] + weights[k] * landed
            return tuple(sums)

        sums = lax.fori_loop(
            0, RELEASES, one_release, (jnp.zeros((depth, LANES), jnp.float32),) * (SCENARIOS * group), unroll=8
        )
        for k in range(group):
            v = [sums[w * group + k] for w in range(SCENARIOS)]
            logs = jnp.log(v[0] * v[1] * (v[2] * v[3])) + jnp.log(v[4] * v[5] * (v[6] * v[7]))
            row = (g * rows + first + k + 1).astype(jnp.float32)
            top = (
                (price_ref[2] / total_depth) * level_c
                + (price_ref[1] / width) * level_b
                + (price_ref[0] / total_rows) * row
            )
            value = -top - (0.5 / SCENARIOS) * logs
            outgoing[t, first + k] = value
            total = total + value
        return total

    def part(n, total):
        step = n // (rows // group)
        q = lax.rem(n, rows // group)

        @pl.when(jnp.logical_and(q == 0, jnp.logical_and(step >= 1, step <= scen_count - 4)))
        def _():
            build_step(scen_count - 2 - step)

        @pl.when(jnp.logical_and(q == 1, step >= 2))
        def _():
            out_copy(step - 1).start()

        return compute(q, step, total)

    total = jnp.zeros((depth, LANES), jnp.float32)
    total = lax.fori_loop(0, scen_count * (rows // group), part, total)

    part_a[...] = jnp.sum(total, axis=0, keepdims=True)
    for step in range(1, scen_count):
        mean_a_copy(step).start()
    out_copy(scen_count - 1).start()
    for step in range(1, scen_count):
        id_copy(step).wait_send()
        tile_copy(step).wait_send()
        side_copy(step).wait_send()
    for step in range(scen_count):
        for way in (0, 1):
            row_copy(step, way).wait_send()
            row_side_copy(step, way).wait_send()
    for step in range(1, scen_count):
        mean_a_copy(step).wait_recv()
    part_b[...] = part_a[...] + jnp.sum(got_a[...], axis=0)
    for step in range(1, NEAR):
        mean_b_copy(step).start()
    result[s] = outgoing[s]
    for step in range(1, scen_count):
        out_copy(step).wait_recv()
        out_copy(step).wait_send()
    for k in range(scen_count):
        avg_ref[:, :, k * LANES : (k + 1) * LANES] = result[k]
    for step in range(1, NEAR):
        mean_b_copy(step).wait_recv()
    part_c[...] = part_b[...] + jnp.sum(got_b[...], axis=0)
    for step in range(1, far_count):
        mean_c_copy(step).start()
    for step in range(1, scen_count):
        mean_a_copy(step).wait_send()
    for step in range(1, NEAR):
        mean_b_copy(step).wait_send()
    for step in range(1, far_count):
        mean_c_copy(step).wait_recv()
    whole = part_c[...] + jnp.sum(got_c[...], axis=0)
    cells = float(total_rows * total_depth * width)
    mean_ref[...] = jnp.broadcast_to(jnp.sum(whole, axis=1, keepdims=True) / cells, (1, LANES))
    for step in range(1, far_count):
        mean_c_copy(step).wait_send()


def solution(mesh):
    scen_count = mesh.shape["scen"]
    grid_count = mesh.shape["grid"]

    def on_device(value_next, scenario_ids, inflow_table, release_shifts, price):
        rows, depth, width = value_next.shape
        dims = (scen_count, grid_count, rows, depth, width)
        reach = rows + 2 * H
        span = depth * (scen_count + 3)
        far_count = grid_count // NEAR
        vmem = pl.BlockSpec(memory_space=pltpu.VMEM)
        dma = pltpu.SemaphoreType.DMA
        peers = scen_count - 1
        f32, i32 = jnp.float32, jnp.int32
        average, mean = pl.pallas_call(
            lambda *refs: kernel(dims, *refs),
            out_shape=(
                jax.ShapeDtypeStruct((rows, depth, width), f32),
                jax.ShapeDtypeStruct((1, LANES), f32),
            ),
            in_specs=[pl.BlockSpec(memory_space=pltpu.HBM)] * 5,
            out_specs=(vmem, vmem),
            scratch_shapes=[
                pltpu.VMEM((rows, depth, width), f32),
                pltpu.VMEM((scen_count, rows // 4, depth, LANES), f32),
                pltpu.VMEM((scen_count, reach, depth, LANES), f32),
                pltpu.VMEM((scen_count, reach // 4, depth, LANES), f32),
                pltpu.VMEM((SHIFTS * reach * span, LANES), f32),
                pltpu.VMEM((scen_count, rows, depth, LANES), f32),
                pltpu.VMEM((scen_count, rows, depth, LANES), f32),
                pltpu.VMEM((1, LANES), i32),
                pltpu.VMEM((scen_count, 1, LANES), i32),
                pltpu.VMEM((1, LANES), f32),
                pltpu.VMEM((peers, 1, LANES), f32),
                pltpu.VMEM((1, LANES), f32),
                pltpu.VMEM((NEAR - 1, 1, LANES), f32),
                pltpu.VMEM((1, LANES), f32),
                pltpu.VMEM((far_count - 1, 1, LANES), f32),
                pltpu.SMEM((scen_count, 1, LANES), i32),
                pltpu.SMEM(scenario_ids.shape, i32),
                pltpu.SMEM(inflow_table.shape[::-1], i32),
                pltpu.SMEM(release_shifts.shape[::-1], i32),
                pltpu.SMEM(price.shape, f32),
                pltpu.SMEM((SCENARIOS * RELEASES,), i32),
                pltpu.SMEM((3 * RELEASES,), f32),
                dma,
                dma((3,)),
                dma((4,)),
                dma((peers,)),
                dma((peers,)),
                dma((peers,)),
                dma((peers,)),
                dma((scen_count, 2)),
                dma((scen_count, 2)),
                dma((scen_count, 2)),
                dma((scen_count, 2)),
                dma((peers,)),
                dma((peers,)),
                dma((peers,)),
                dma((peers,)),
                dma((peers,)),
                dma((peers,)),
                dma((NEAR - 1,)),
                dma((NEAR - 1,)),
                dma((far_count - 1,)),
                dma((far_count - 1,)),
            ],
            compiler_params=pltpu.CompilerParams(
                collective_id=0, has_side_effects=True, vmem_limit_bytes=53 * 1024 * 1024
            ),
        )(value_next, scenario_ids, inflow_table.T, release_shifts.T, price)
        return average - mean[0, 0]

    return jax.shard_map(
        on_device,
        mesh=mesh,
        in_specs=(P("grid", "scen", None), P("scen"), P(), P(), P()),
        out_specs=P("grid", "scen", None),
        check_vma=False,
    )
```
